32 devices in a mesh: dp: 2 (over core), fsdp: 16 (over z, y, x).
Axes of the slice: x: 2, y: 2, z: 4, core: 2. Of those that a mesh axis runs over, the one named last changes fastest.
Arguments:
- tokens: bfloat16 [32, 128, 768], P(('dp', 'fsdp')), may hold values from -6 to 6
- cotangent: bfloat16 [32, 128, 768], P(('dp', 'fsdp')), may hold values from -6 to 6
- lengths: int32 [32, 2], P(('dp', 'fsdp')), may hold values from 1 to 128, as said below
- joint_weight: bfloat16 [1, 768, 2304], P(None, 'fsdp'), may hold values from -0.21875 to 0.21875
- output_weight: bfloat16 [1, 768, 768], P(None, 'fsdp'), may hold values from -0.875 to 0.875
- expand_weight: bfloat16 [1, 768, 3072], P(None, 'fsdp'), may hold values from -0.21875 to 0.21875
- shrink_weight: bfloat16 [1, 3072, 768], P(None, 'fsdp'), may hold values from -0.109375 to 0.109375
- norm_gains: bfloat16 [1, 2, 768], P(None, None, 'fsdp'), may hold values from 0.5 to 1.5
- bias_rows: bfloat16 [1, 10, 768], P(None, None, 'fsdp'), may hold values from -2 to 2
- master_joint: float32 [1, 768, 2304], P(None, 'fsdp', 'dp'), may hold values from -0.21875 to 0.21875
- master_output: float32 [1, 768, 768], P(None, 'fsdp', 'dp'), may hold values from -0.875 to 0.875
- master_expand: float32 [1, 768, 3072], P(None, 'fsdp', 'dp'), may hold values from -0.21875 to 0.21875
- master_shrink: float32 [1, 3072, 768], P(None, 'fsdp', 'dp'), may hold values from -0.109375 to 0.109375
- master_gains: float32 [1, 2, 768], P(None, None, 'fsdp'), may hold values from 0.5 to 1.5
- master_biases: float32 [1, 10, 768], P(None, None, 'fsdp'), may hold values from -2 to 2
- first_joint: float32 [1, 768, 2304], P(None, 'fsdp', 'dp'), may hold values from -192 to 192
- first_output: float32 [1, 768, 768], P(None, 'fsdp', 'dp'), may hold values from -192 to 192
- first_expand: float32 [1, 768, 3072], P(None, 'fsdp', 'dp'), may hold values from -192 to 192
- first_shrink: float32 [1, 3072, 768], P(None, 'fsdp', 'dp'), may hold values from -192 to 192
- first_gains: float32 [1, 2, 768], P(None, None, 'fsdp'), may hold values from -192 to 192
- first_biases: float32 [1, 10, 768], P(None, None, 'fsdp'), may hold values from -192 to 192
- second_joint: float32 [1, 768, 2304], P(None, 'fsdp', 'dp'), may hold values from 204.8 to 8192
- second_output: float32 [1, 768, 768], P(None, 'fsdp', 'dp'), may hold values from 204.8 to 8192
- second_expand: float32 [1, 768, 3072], P(None, 'fsdp', 'dp'), may hold values from 204.8 to 8192
- second_shrink: float32 [1, 3072, 768], P(None, 'fsdp', 'dp'), may hold values from 204.8 to 8192
- second_gains: float32 [1, 2, 768], P(None, None, 'fsdp'), may hold values from 204.8 to 8192
- second_biases: float32 [1, 10, 768], P(None, None, 'fsdp'), may hold values from 204.8 to 8192
Outputs:
- output_rows: float32 [32, 128, 768], P(('dp', 'fsdp'))
- input_grad: float32 [32, 128, 768], P(('dp', 'fsdp'))
- grad_joint: float32 [1, 768, 2304], P(None, 'fsdp', 'dp')
- new_master_joint: float32 [1, 768, 2304], P(None, 'fsdp', 'dp')
- new_first_joint: float32 [1, 768, 2304], P(None, 'fsdp', 'dp')
- new_second_joint: float32 [1, 768, 2304], P(None, 'fsdp', 'dp')
- new_copy_joint: bfloat16 [1, 768, 2304], P(None, 'fsdp', 'dp')
- grad_output: float32 [1, 768, 768], P(None, 'fsdp', 'dp')
- new_master_output: float32 [1, 768, 768], P(None, 'fsdp', 'dp')
- new_first_output: float32 [1, 768, 768], P(None, 'fsdp', 'dp')
- new_second_output: float32 [1, 768, 768], P(None, 'fsdp', 'dp')
- new_copy_output: bfloat16 [1, 768, 768], P(None, 'fsdp', 'dp')
- grad_expand: float32 [1, 768, 3072], P(None, 'fsdp', 'dp')
- new_master_expand: float32 [1, 768, 3072], P(None, 'fsdp', 'dp')
- new_first_expand: float32 [1, 768, 3072], P(None, 'fsdp', 'dp')
- new_second_expand: float32 [1, 768, 3072], P(None, 'fsdp', 'dp')
- new_copy_expand: bfloat16 [1, 768, 3072], P(None, 'fsdp', 'dp')
- grad_shrink: float32 [1, 3072, 768], P(None, 'fsdp', 'dp')
- new_master_shrink: float32 [1, 3072, 768], P(None, 'fsdp', 'dp')
- new_first_shrink: float32 [1, 3072, 768], P(None, 'fsdp', 'dp')
- new_second_shrink: float32 [1, 3072, 768], P(None, 'fsdp', 'dp')
- new_copy_shrink: bfloat16 [1, 3072, 768], P(None, 'fsdp', 'dp')
- grad_gains: float32 [1, 2, 768], P(None, None, 'fsdp')
- new_master_gains: float32 [1, 2, 768], P(None, None, 'fsdp')
- new_first_gains: float32 [1, 2, 768], P(None, None, 'fsdp')
- new_second_gains: float32 [1, 2, 768], P(None, None, 'fsdp')
- new_copy_gains: bfloat16 [1, 2, 768], P(None, None, 'fsdp')
- grad_biases: float32 [1, 10, 768], P(None, None, 'fsdp')
- new_master_biases: float32 [1, 10, 768], P(None, None, 'fsdp')
- new_first_biases: float32 [1, 10, 768], P(None, None, 'fsdp')
- new_second_biases: float32 [1, 10, 768], P(None, None, 'fsdp')
- new_copy_biases: bfloat16 [1, 10, 768], P(None, None, 'fsdp')
The draws below stay inside these ranges and needn't reach their ends.
Inputs may be any that keep to these rules, and one draw needn't show every extreme that they name: `lengths`: column 0 of an item's row is its prefix length, 1 to its total; column 1 is its total filled length, 32 to 128; some item fills all 128 slots.
All inputs are finite; a program needn't handle non-finite values.
Results may differ from the reference program's by a relative error of at most 0.012.
Values may be sent and summed in bfloat16 or wider, within the bound.
No kernel may reach another device: no remote copies, remote signals or barrier semaphores. Data moves between devices by JAX's collectives and lax.ppermute only.
A program may use at most 128 MiB of HBM per device.

```python
import math
import jax
import jax.numpy as jnp
from jax import lax

D = 768
HEAD_DIM = 64
FF = 3072
LAYERS = 1
STEP_COUNT = 3
SEQ = 128
ITEMS = 32


def draw_lengths(key, part):
    first_key, second_key, third_key = jax.random.split(key, 3)
    totals = jax.random.randint(first_key, (ITEMS,), SEQ // 4, SEQ + 1)
    chosen = jax.random.randint(second_key, (), 0, ITEMS)
    totals = jnp.where(jnp.arange(ITEMS) == chosen, SEQ, totals)
    prefix = 1 + jax.random.randint(third_key, (ITEMS,), 0, 1 << 20) % totals
    return jnp.stack([prefix, totals], axis=1).astype(jnp.int32)


def shard_levels(stream_key, dims, shards, low, high):
    level, own = 1.0, jax.random.fold_in(stream_key, 6)
    for axis_at, parts in shards:
        steps = jnp.exp(jax.random.uniform(jax.random.fold_in(own, axis_at), (parts,), jnp.float32, low / len(shards), high / len(shards)))
        level = level * jnp.repeat(steps, dims[axis_at] // parts).reshape([-1 if axis == axis_at else 1 for axis in range(len(dims))])
    return level


def scatter_about(stream_key, extent, width, limit, cuts=(), kind=jnp.bfloat16):
    level = shard_levels(stream_key, extent, cuts, -0.22, 0.18) if cuts else 1.0
    values = jax.random.normal(stream_key, extent, jnp.float32) * width * level
    return jnp.minimum(jnp.maximum(values, -limit), limit).astype(kind)


def setup_inputs(seed: int = 0) -> dict:
    key_of = jax.random.split(jax.random.key(seed), 28)
    return {
        "tokens": scatter_about(key_of[0], (ITEMS, SEQ, D), 1.0, 6.0, ((0, 32),)),
        "cotangent": scatter_about(key_of[1], (ITEMS, SEQ, D), 1.0, 6.0, ((0, 32),)),
        "lengths": draw_lengths(jax.random.fold_in(key_of[27], 71), 0),
        "joint_weight": scatter_about(key_of[3], (LAYERS, D, 3 * D), D ** -0.5, 0.21875, ((1, 16),)),
        "output_weight": scatter_about(key_of[4], (LAYERS, D, D), (D // 16) ** -0.5, 0.875, ((1, 16),)),
        "expand_weight": scatter_about(key_of[5], (LAYERS, D, FF), D ** -0.5, 0.21875, ((1, 16),)),
        "shrink_weight": scatter_about(key_of[6], (LAYERS, FF, D), FF ** -0.5, 0.109375, ((1, 16),)),
        "norm_gains": jnp.clip(1.0 + 0.1 * jax.random.normal(key_of[7], (LAYERS, 2, D), jnp.float32), 0.5, 1.5).astype(jnp.bfloat16),
        "bias_rows": scatter_about(key_of[8], (LAYERS, 6 + FF // D, D), 0.3, 2.0, ((2, 16),)),
        "master_joint": scatter_about(key_of[9], (LAYERS, D, 3 * D), D ** -0.5, 0.21875, ((1, 16), (2, 2)), jnp.float32),
        "master_output": scatter_about(key_of[10], (LAYERS, D, D), (D // 16) ** -0.5, 0.875, ((1, 16), (2, 2)), jnp.float32),
        "master_expand": scatter_about(key_of[11], (LAYERS, D, FF), D ** -0.5, 0.21875, ((1, 16), (2, 2)), jnp.float32),
        "master_shrink": scatter_about(key_of[12], (LAYERS, FF, D), FF ** -0.5, 0.109375, ((1, 16), (2, 2)), jnp.float32),
        "master_gains": jnp.clip(1.0 + 0.1 * jax.random.normal(key_of[13], (LAYERS, 2, D), jnp.float32), 0.5, 1.5),
        "master_biases": scatter_about(key_of[14], (LAYERS, 6 + FF // D, D), 0.3, 2.0, ((2, 16),), jnp.float32),
        "first_joint": scatter_about(key_of[15], (LAYERS, D, 3 * D), (0.5 * (ITEMS * SEQ) ** 0.5), 192.0, ((1, 16), (2, 2)), jnp.float32),
        "first_output": scatter_about(key_of[16], (LAYERS, D, D), (0.5 * (ITEMS * SEQ) ** 0.5), 192.0, ((1, 16), (2, 2)), jnp.float32),
        "first_expand": scatter_about(key_of[17], (LAYERS, D, FF), (0.5 * (ITEMS * SEQ) ** 0.5), 192.0, ((1, 16), (2, 2)), jnp.float32),
        "first_shrink": scatter_about(key_of[18], (LAYERS, FF, D), (0.5 * (ITEMS * SEQ) ** 0.5), 192.0, ((1, 16), (2, 2)), jnp.float32),
        "first_gains": scatter_about(key_of[19], (LAYERS, 2, D), (0.5 * (ITEMS * SEQ) ** 0.5), 192.0, ((2, 16),), jnp.float32),
        "first_biases": scatter_about(key_of[20], (LAYERS, 6 + FF // D, D), (0.5 * (ITEMS * SEQ) ** 0.5), 192.0, ((2, 16),), jnp.float32),
        "second_joint": jnp.clip(jnp.exp(math.log(8192.0) - 3.6888794 * jax.random.uniform(key_of[21], (LAYERS, D, 3 * D), jnp.float32) ** shard_levels(key_of[21], (LAYERS, D, 3 * D), ((1, 16), (2, 2)), -0.2, 0.2)), 204.8, 8192.0),
        "second_output": jnp.clip(jnp.exp(math.log(8192.0) - 3.6888794 * jax.random.uniform(key_of[22], (LAYERS, D, D), jnp.float32) ** shard_levels(key_of[22], (LAYERS, D, D), ((1, 16), (2, 2)), -0.2, 0.2)), 204.8, 8192.0),
        "second_expand": jnp.clip(jnp.exp(math.log(8192.0) - 3.6888794 * jax.random.uniform(key_of[23], (LAYERS, D, FF), jnp.float32) ** shard_levels(key_of[23], (LAYERS, D, FF), ((1, 16), (2, 2)), -0.2, 0.2)), 204.8, 8192.0),
        "second_shrink": jnp.clip(jnp.exp(math.log(8192.0) - 3.6888794 * jax.random.uniform(key_of[24], (LAYERS, FF, D), jnp.float32) ** shard_levels(key_of[24], (LAYERS, FF, D), ((1, 16), (2, 2)), -0.2, 0.2)), 204.8, 8192.0),
        "second_gains": jnp.clip(jnp.exp(math.log(8192.0) - 3.6888794 * jax.random.uniform(key_of[25], (LAYERS, 2, D), jnp.float32) ** shard_levels(key_of[25], (LAYERS, 2, D), ((2, 16),), -0.2, 0.2)), 204.8, 8192.0),
        "second_biases": jnp.clip(jnp.exp(math.log(8192.0) - 3.6888794 * jax.random.uniform(key_of[26], (LAYERS, 6 + FF // D, D), jnp.float32) ** shard_levels(key_of[26], (LAYERS, 6 + FF // D, D), ((2, 16),), -0.2, 0.2)), 204.8, 8192.0),
    }


@jax.custom_vjp
def low(v):
    return lax.optimization_barrier(v.astype(jnp.bfloat16)).astype(jnp.float32)

@jax.custom_vjp
def low_back(v):
    return v

def low_keep(v):
    return (low(v), None)

def low_pass(kept, grad):
    return (grad,)

def back_keep(v):
    return (v, None)

def back_low(kept, grad):
    return (low(grad),)
low.defvjp(low_keep, low_pass)
low_back.defvjp(back_keep, back_low)
beta_one = 0.5
beta_two = 0.5
learning_rate = 0.02
small_rate = 0.25
weight_decay = 0.1
epsilon = 1e-08
norm_epsilon = 1e-05

def matmul(left, right):
    return jnp.dot(left, right, precision=lax.Precision.HIGHEST, preferred_element_type=jnp.float32)

def layer_norm(stream, gain, shift):
    centred = stream - lax.optimization_barrier(jnp.mean(stream, axis=-1, keepdims=True))
    spread = lax.optimization_barrier(jnp.mean(centred * centred, axis=-1, keepdims=True))
    return centred * lax.rsqrt(spread + norm_epsilon) * gain + shift

def visible_mask(prefix, total, token_count):
    position = jnp.arange(token_count, dtype=jnp.int32)
    query_pos = position[:, None]
    key_pos = position[None, :]
    return (key_pos < total) & ((key_pos <= query_pos) | (key_pos < prefix))

def softmax_rows(scores, visible):
    return jax.nn.softmax(jnp.where(visible[None], scores, -1e+30), axis=-1)

def block(stream, joint_mat, output, expand, shrink, gain_rows, biases, visible):
    token_count, model_width = stream.shape
    head_count = model_width // HEAD_DIM
    score_scale = HEAD_DIM ** (-0.5)
    normed = low(layer_norm(stream, gain_rows[0], biases[0]))
    joint_bias = jnp.concatenate([biases[2], jnp.zeros_like(biases[2]), biases[3]])
    projected = low(low_back(matmul(normed, joint_mat) + joint_bias))
    queries = projected[:, :model_width].reshape(token_count, head_count, HEAD_DIM)
    key_rows = projected[:, model_width:2 * model_width].reshape(token_count, head_count, HEAD_DIM)
    values = projected[:, 2 * model_width:].reshape(token_count, head_count, HEAD_DIM)
    dot_scores = jnp.einsum('qhd,khd->hqk', queries, key_rows, precision=lax.Precision.HIGHEST)
    attention = low(softmax_rows(low_back(dot_scores) * score_scale, visible))
    attended = jnp.einsum('hqk,khd->qhd', attention, values, precision=lax.Precision.HIGHEST)
    attended = low(low_back(attended.reshape(token_count, model_width)))
    branch = low_back(matmul(attended, output) + biases[4])
    middle = stream + branch
    normed_two = low(layer_norm(middle, gain_rows[1], biases[1]))
    hidden = low_back(matmul(normed_two, expand) + biases[6:].reshape(-1))
    active = low(jax.nn.gelu(hidden, approximate=True))
    second = low_back(matmul(active, shrink) + biases[5])
    return middle + second

def adamw(master, first, second, gradient, rate):
    first_new = beta_one * first + (1.0 - beta_one) * gradient
    second_new = beta_two * second + (1.0 - beta_two) * gradient * gradient
    first_hat = first_new / (1.0 - beta_one ** STEP_COUNT)
    second_hat = second_new / (1.0 - beta_two ** STEP_COUNT)
    master_new = master - rate * (first_hat / (jnp.sqrt(second_hat) + epsilon) + weight_decay * master)
    return (master_new, first_new, second_new, master_new.astype(jnp.bfloat16))

def reference(tokens, cotangent, lengths, joint_weight, output_weight, expand_weight, shrink_weight, norm_gains, bias_rows, master_joint, master_output, master_expand, master_shrink, master_gains, master_biases, first_joint, first_output, first_expand, first_shrink, first_gains, first_biases, second_joint, second_output, second_expand, second_shrink, second_gains, second_biases):
    params = tuple((weight.astype(jnp.float32) for weight in (joint_weight, output_weight, expand_weight, shrink_weight, norm_gains, bias_rows)))

    def forward(stream, weights, visible):
        for layer_index in range(LAYERS):
            stream = block(stream, weights[0][layer_index], weights[1][layer_index], weights[2][layer_index], weights[3][layer_index], weights[4][layer_index], weights[5][layer_index], visible)
        return stream

    def per_item(running, item):
        stream, upstream, meta = item
        visible = visible_mask(meta[0], meta[1], stream.shape[0])
        result, pull_back = jax.vjp(lambda inputs, weights: forward(inputs, weights, visible), stream.astype(jnp.float32), params)
        grad_stream, grad_params = pull_back(upstream.astype(jnp.float32))
        running = tuple((held + addend for held, addend in zip(running, grad_params)))
        return (running, (result, grad_stream))
    zeros_init = tuple((jnp.zeros(weight.shape, jnp.float32) for weight in params))
    grads, (output_rows, input_grad) = lax.scan(per_item, zeros_init, (tokens, cotangent, lengths))
    mj, fj, sj, cj = adamw(master_joint, first_joint, second_joint, grads[0], learning_rate)
    mo, fo, so, co = adamw(master_output, first_output, second_output, grads[1], learning_rate)
    me, fe, se, ce = adamw(master_expand, first_expand, second_expand, grads[2], learning_rate)
    ms, fs, ss, cs = adamw(master_shrink, first_shrink, second_shrink, grads[3], learning_rate)
    mg, fg, sg, cg = adamw(master_gains, first_gains, second_gains, grads[4], small_rate)
    mb, fb, sb, cb = adamw(master_biases, first_biases, second_biases, grads[5], small_rate)
    return (output_rows, input_grad, grads[0], mj, fj, sj, cj, grads[1], mo, fo, so, co, grads[2], me, fe, se, ce, grads[3], ms, fs, ss, cs, grads[4], mg, fg, sg, cg, grads[5], mb, fb, sb, cb)
```

```python
import jax
import jax.numpy as jnp
from jax import lax
from jax.sharding import PartitionSpec as P

HEAD_DIM = 64
STEP_COUNT = 3


beta_one = 0.5
beta_two = 0.5
learning_rate = 0.02
small_rate = 0.25
weight_decay = 0.1
epsilon = 1e-08
norm_epsilon = 1e-05


def layer_norm(stream, gain, shift):
    centred = stream - jnp.mean(stream, axis=-1, keepdims=True)
    spread = jnp.mean(centred * centred, axis=-1, keepdims=True)
    return centred * lax.rsqrt(spread + norm_epsilon) * gain + shift


def visible_mask(prefix, total, token_count):
    position = jnp.arange(token_count, dtype=jnp.int32)
    query_pos = position[:, None]
    key_pos = position[None, :]
    return (key_pos < total) & ((key_pos <= query_pos) | (key_pos < prefix))


def softmax_rows(scores, visible):
    return jax.nn.softmax(jnp.where(visible[None], scores, -1e30), axis=-1)


def outer_sum(left, right):
    return lax.dot_general(
        left, right, (((0,), (0,)), ((), ())), preferred_element_type=jnp.float32
    )


def times_back(left, right):
    return lax.dot_general(
        left, right, (((1,), (1,)), ((), ())), preferred_element_type=jnp.float32
    )


def layer_parts(stream, gathered, visible):
    joint_mat, output, expand, shrink, gain_rows, biases = gathered
    token_count, model_width = stream.shape
    head_count = model_width // HEAD_DIM
    gain_full = gain_rows.astype(jnp.float32)
    bias_full = biases.astype(jnp.float32)
    normed = layer_norm(stream, gain_full[0], bias_full[0]).astype(jnp.bfloat16)
    joint_bias = jnp.concatenate([bias_full[2], jnp.zeros_like(bias_full[2]), bias_full[3]])
    projected = (
        jnp.dot(normed, joint_mat, preferred_element_type=jnp.float32) + joint_bias
    ).astype(jnp.bfloat16)
    queries = projected[:, :model_width].reshape(token_count, head_count, HEAD_DIM)
    key_rows = projected[:, model_width : 2 * model_width].reshape(
        token_count, head_count, HEAD_DIM
    )
    values = projected[:, 2 * model_width :].reshape(token_count, head_count, HEAD_DIM)
    dot_scores = jnp.einsum("qhd,khd->hqk", queries, key_rows, preferred_element_type=jnp.float32)
    scaled = dot_scores * HEAD_DIM ** (-0.5)
    attend_low = softmax_rows(scaled, visible).astype(jnp.bfloat16)
    attended = jnp.einsum("hqk,khd->qhd", attend_low, values, preferred_element_type=jnp.float32)
    attended = attended.reshape(token_count, model_width).astype(jnp.bfloat16)
    branch = jnp.dot(attended, output, preferred_element_type=jnp.float32) + bias_full[4]
    middle = stream + branch
    normed_two = layer_norm(middle, gain_full[1], bias_full[1]).astype(jnp.bfloat16)
    hidden = jnp.dot(normed_two, expand, preferred_element_type=jnp.float32) + bias_full[
        6:
    ].reshape(-1)
    active = jax.nn.gelu(hidden, approximate=True).astype(jnp.bfloat16)
    second = jnp.dot(active, shrink, preferred_element_type=jnp.float32) + bias_full[5]
    kept = (normed, projected, scaled, attend_low, attended, middle, normed_two, hidden, active)
    return (middle + second, kept)


def layer_both(stream, gathered, visible, upstream):
    joint_mat, output, expand, shrink, gain_rows, biases = gathered
    token_count, model_width = stream.shape
    head_count = model_width // HEAD_DIM
    score_scale = HEAD_DIM ** (-0.5)
    gain_full = gain_rows.astype(jnp.float32)
    bias_full = biases.astype(jnp.float32)
    result, kept = layer_parts(stream, gathered, visible)
    normed, projected, scaled, attend_low, attended, middle, normed_two, hidden, active = kept
    queries = projected[:, :model_width].reshape(token_count, head_count, HEAD_DIM)
    key_rows = projected[:, model_width : 2 * model_width].reshape(
        token_count, head_count, HEAD_DIM
    )
    values = projected[:, 2 * model_width :].reshape(token_count, head_count, HEAD_DIM)
    back_second = upstream.astype(jnp.bfloat16)
    grad_shrink = outer_sum(active, back_second)
    bias_shrink = jnp.sum(back_second.astype(jnp.float32), axis=0)
    back_active = times_back(back_second, shrink)
    gelu_value, gelu_pull = jax.vjp(lambda inner: jax.nn.gelu(inner, approximate=True), hidden)
    back_hidden = gelu_pull(back_active)[0].astype(jnp.bfloat16)
    grad_expand = outer_sum(normed_two, back_hidden)
    bias_expand = jnp.sum(back_hidden.astype(jnp.float32), axis=0)
    back_normed_two = times_back(back_hidden, expand)
    norm_value, norm_pull = jax.vjp(layer_norm, middle, gain_full[1], bias_full[1])
    back_inner, gain_two, shift_two = norm_pull(back_normed_two)
    back_middle = upstream + back_inner
    back_branch = back_middle.astype(jnp.bfloat16)
    grad_output = outer_sum(attended, back_branch)
    bias_output = jnp.sum(back_branch.astype(jnp.float32), axis=0)
    back_attended = (
        times_back(back_branch, output)
        .astype(jnp.bfloat16)
        .reshape(token_count, head_count, HEAD_DIM)
    )
    grad_values = jnp.einsum(
        "hqk,qhd->khd", attend_low, back_attended, preferred_element_type=jnp.float32
    )
    back_attention = jnp.einsum(
        "qhd,khd->hqk", back_attended, values, preferred_element_type=jnp.float32
    )
    soft_value, soft_pull = jax.vjp(lambda inner: softmax_rows(inner, visible), scaled)
    back_scores = (soft_pull(back_attention)[0] * score_scale).astype(jnp.bfloat16)
    grad_queries = jnp.einsum(
        "hqk,khd->qhd", back_scores, key_rows, preferred_element_type=jnp.float32
    )
    grad_keys = jnp.einsum("hqk,qhd->khd", back_scores, queries, preferred_element_type=jnp.float32)
    back_projected = jnp.concatenate(
        [
            grad_queries.reshape(token_count, model_width),
            grad_keys.reshape(token_count, model_width),
            grad_values.reshape(token_count, model_width),
        ],
        axis=1,
    ).astype(jnp.bfloat16)
    grad_joint = outer_sum(normed, back_projected)
    project_wide = back_projected.astype(jnp.float32)
    bias_query = jnp.sum(project_wide[:, :model_width], axis=0)
    bias_value = jnp.sum(project_wide[:, 2 * model_width :], axis=0)
    back_normed = times_back(back_projected, joint_mat)
    first_value, first_pull = jax.vjp(layer_norm, stream, gain_full[0], bias_full[0])
    back_stream, gain_one, shift_one = first_pull(back_normed)
    gain_grad = jnp.stack([gain_one, gain_two])
    bias_grad = jnp.concatenate(
        [
            jnp.stack([shift_one, shift_two, bias_query, bias_value, bias_output, bias_shrink]),
            bias_expand.reshape(-1, model_width),
        ]
    )
    return (
        result,
        back_middle + back_stream,
        (grad_joint, grad_output, grad_expand, grad_shrink, gain_grad, bias_grad),
    )


def adamw(master, first, second, gradient, rate):
    first_new = beta_one * first + (1.0 - beta_one) * gradient
    second_new = beta_two * second + (1.0 - beta_two) * gradient * gradient
    first_hat = first_new / (1.0 - beta_one**STEP_COUNT)
    second_hat = second_new / (1.0 - beta_two**STEP_COUNT)
    master_new = master - rate * (
        first_hat / (jnp.sqrt(second_hat) + epsilon) + weight_decay * master
    )
    return (master_new, first_new, second_new, master_new.astype(jnp.bfloat16))


def bit_plan(size):
    bits = size.bit_length() - 1
    side = bits // 3
    x_bits = tuple(range(side))
    y_bits = tuple(range(side, 2 * side))
    z_bits = tuple(range(2 * side, bits))
    return x_bits, y_bits, z_bits


def swap(value, bit, size):
    return lax.ppermute(value, "fsdp", [(i, i ^ (1 << bit)) for i in range(size)])


def swap_core(value):
    return lax.ppermute(value, "dp", [(0, 1), (1, 0)])


def gather_bits(value, bits, held, index, size):
    held = list(held)
    for bit in bits:
        other = swap(value, bit, size)
        mine = ((index >> bit) & 1) == 0
        spot = sum(1 for kept in held if kept > bit)
        low = jnp.where(mine, value, other)
        high = jnp.where(mine, other, value)
        value = jnp.stack([low, high], axis=spot)
        held.append(bit)
    return value, held


def gather_weight(shard, index, core, size):
    x_bits, y_bits, z_bits = bit_plan(size)
    rows, width = shard.shape
    half = width // 2
    mine = lax.dynamic_slice_in_dim(shard, core * half, half, axis=1)
    depth, held = gather_bits(mine, z_bits, (), index, size)
    lead = len(held)
    one = lax.slice_in_dim(depth, 0, rows // 2, axis=lead)
    two = lax.slice_in_dim(depth, rows // 2, rows, axis=lead)
    one, held_one = gather_bits(one, x_bits + y_bits, held, index, size)
    two, held_two = gather_bits(two, y_bits + x_bits, held, index, size)
    whole = jnp.concatenate([one, two], axis=len(held_one)).reshape(size * rows, half)
    other = swap_core(whole)
    return jnp.concatenate(
        [jnp.where(core == 0, whole, other), jnp.where(core == 0, other, whole)], axis=1
    )


def scatter_bits(value, bits, held, index, size, last=False):
    held = list(held)
    for place, bit in enumerate(bits):
        spot = sum(1 for kept in held if kept > bit)
        mine = (index >> bit) & 1
        keep = lax.dynamic_index_in_dim(value, mine, axis=spot, keepdims=False)
        send = lax.dynamic_index_in_dim(value, 1 - mine, axis=spot, keepdims=False)
        got = swap(send, bit, size)
        value = keep.astype(jnp.float32) + got.astype(jnp.float32)
        held.remove(bit)
        if not (last and place == len(bits) - 1):
            value = value.astype(jnp.bfloat16)
    return value, held


def scatter_grad(grad, index, core, size):
    x_bits, y_bits, z_bits = bit_plan(size)
    total_rows, width = grad.shape
    rows = total_rows // size
    half = width // 2
    keep = lax.dynamic_slice_in_dim(grad, core * half, half, axis=1)
    send = lax.dynamic_slice_in_dim(grad, (1 - core) * half, half, axis=1)
    got = swap_core(send)
    value = (keep.astype(jnp.float32) + got.astype(jnp.float32)).astype(jnp.bfloat16)
    bits = len(x_bits) + len(y_bits) + len(z_bits)
    value = value.reshape((2,) * bits + (rows, half))
    held = list(range(bits))
    one = lax.slice_in_dim(value, 0, rows // 2, axis=bits)
    two = lax.slice_in_dim(value, rows // 2, rows, axis=bits)
    one, held_one = scatter_bits(one, y_bits + x_bits, held, index, size)
    two, held_two = scatter_bits(two, x_bits + y_bits, held, index, size)
    both = jnp.concatenate([one, two], axis=len(held_one))
    result, _ = scatter_bits(both, tuple(reversed(z_bits)), held_one, index, size, last=True)
    return result


def sum_all(value, size):
    value = value + swap_core(value)
    bits = size.bit_length() - 1
    for bit in range(bits):
        value = value + swap(value, bit, size)
    return value


def join_small(gains, biases, index, size):
    piece = jnp.concatenate([gains, biases], axis=0)
    rows, width = piece.shape
    room = jnp.zeros((rows, width * size), piece.dtype)
    value = lax.dynamic_update_slice(room, piece, (0, index * width))
    bits = size.bit_length() - 1
    for bit in range(bits):
        value = value + swap(value, bit, size)
    return value


def local(
    tokens,
    cotangent,
    lengths,
    joint_weight,
    output_weight,
    expand_weight,
    shrink_weight,
    norm_gains,
    bias_rows,
    master_joint,
    master_output,
    master_expand,
    master_shrink,
    master_gains,
    master_biases,
    first_joint,
    first_output,
    first_expand,
    first_shrink,
    first_gains,
    first_biases,
    second_joint,
    second_output,
    second_expand,
    second_shrink,
    second_gains,
    second_biases,
):
    size = lax.axis_size("fsdp")
    index = lax.axis_index("fsdp")
    core = lax.axis_index("dp")
    stream = tokens[0].astype(jnp.float32)
    visible = visible_mask(lengths[0, 0], lengths[0, 1], stream.shape[0])
    small = join_small(norm_gains[0], bias_rows[0], index, size)
    gathered = (
        gather_weight(joint_weight[0], index, core, size),
        gather_weight(output_weight[0], index, core, size),
        gather_weight(expand_weight[0], index, core, size),
        gather_weight(shrink_weight[0], index, core, size),
        small[:2],
        small[2:],
    )
    upstream = cotangent[0].astype(jnp.float32)
    result, input_grad, layer_grads = layer_both(stream, gathered, visible, upstream)
    matrix_sums = tuple(
        scatter_grad(layer_grads[place].astype(jnp.bfloat16), index, core, size)
        for place in range(4)
    )
    small_grads = sum_all(jnp.concatenate([layer_grads[4], layer_grads[5]], axis=0), size)
    width = norm_gains.shape[2]
    small_own = lax.dynamic_slice_in_dim(small_grads, index * width, width, axis=1)
    masters = (
        master_joint,
        master_output,
        master_expand,
        master_shrink,
        master_gains,
        master_biases,
    )
    firsts = (first_joint, first_output, first_expand, first_shrink, first_gains, first_biases)
    seconds = (
        second_joint,
        second_output,
        second_expand,
        second_shrink,
        second_gains,
        second_biases,
    )
    totals_all = tuple(value[None] for value in matrix_sums) + (
        small_own[None, :2],
        small_own[None, 2:],
    )
    results = [result[None], input_grad[None]]
    for group_index in range(6):
        group_rate = learning_rate if group_index < 4 else small_rate
        new_master, new_first, new_second, new_copy = adamw(
            masters[group_index],
            firsts[group_index],
            seconds[group_index],
            totals_all[group_index],
            group_rate,
        )
        results.extend([totals_all[group_index], new_master, new_first, new_second, new_copy])
    return tuple(results)


def solution(mesh):
    placed = (
        P(("dp", "fsdp"), None, None),
        P(("dp", "fsdp"), None, None),
        P(("dp", "fsdp"), None),
        P(None, "fsdp", None),
        P(None, "fsdp", None),
        P(None, "fsdp", None),
        P(None, "fsdp", None),
        P(None, None, "fsdp"),
        P(None, None, "fsdp"),
        P(None, "fsdp", "dp"),
        P(None, "fsdp", "dp"),
        P(None, "fsdp", "dp"),
        P(None, "fsdp", "dp"),
        P(None, None, "fsdp"),
        P(None, None, "fsdp"),
        P(None, "fsdp", "dp"),
        P(None, "fsdp", "dp"),
        P(None, "fsdp", "dp"),
        P(None, "fsdp", "dp"),
        P(None, None, "fsdp"),
        P(None, None, "fsdp"),
        P(None, "fsdp", "dp"),
        P(None, "fsdp", "dp"),
        P(None, "fsdp", "dp"),
        P(None, "fsdp", "dp"),
        P(None, None, "fsdp"),
        P(None, None, "fsdp"),
    )
    return jax.shard_map(
        local,
        mesh=mesh,
        in_specs=placed,
        out_specs=(
            P(("dp", "fsdp"), None, None),
            P(("dp", "fsdp"), None, None),
            P(None, "fsdp", "dp"),
            P(None, "fsdp", "dp"),
            P(None, "fsdp", "dp"),
            P(None, "fsdp", "dp"),
            P(None, "fsdp", "dp"),
            P(None, "fsdp", "dp"),
            P(None, "fsdp", "dp"),
            P(None, "fsdp", "dp"),
            P(None, "fsdp", "dp"),
            P(None, "fsdp", "dp"),
            P(None, "fsdp", "dp"),
            P(None, "fsdp", "dp"),
            P(None, "fsdp", "dp"),
            P(None, "fsdp", "dp"),
            P(None, "fsdp", "dp"),
            P(None, "fsdp", "dp"),
            P(None, "fsdp", "dp"),
            P(None, "fsdp", "dp"),
            P(None, "fsdp", "dp"),
            P(None, "fsdp", "dp"),
            P(None, None, "fsdp"),
            P(None, None, "fsdp"),
            P(None, None, "fsdp"),
            P(None, None, "fsdp"),
            P(None, None, "fsdp"),
            P(None, None, "fsdp"),
            P(None, None, "fsdp"),
            P(None, None, "fsdp"),
            P(None, None, "fsdp"),
            P(None, None, "fsdp"),
        ),
        check_vma=False,
    )
```

```python
import jax
import jax.numpy as jnp
from jax import lax
from jax.experimental import pallas as pl
from jax.experimental.pallas import tpu as pltpu
from jax.sharding import PartitionSpec as P

HEAD_DIM = 64
STEP_COUNT = 3


beta_one = 0.5
beta_two = 0.5
learning_rate = 0.02
small_rate = 0.25
weight_decay = 0.1
epsilon = 1e-08
norm_epsilon = 1e-05
curve = 0.7978845608028654
cubic = 0.044715
half_type = jnp.bfloat16
wide = jnp.float32


def matmul(left, right):
    return lax.dot_general(left, right, (((1,), (0,)), ((), ())), preferred_element_type=wide)


def outer_sum(left, right):
    return lax.dot_general(left, right, (((0,), (0,)), ((), ())), preferred_element_type=wide)


def times_back(left, right):
    return lax.dot_general(left, right, (((1,), (1,)), ((), ())), preferred_element_type=wide)


def norm_parts(stream):
    centred = stream - jnp.mean(stream, axis=-1, keepdims=True)
    spread = jnp.mean(centred * centred, axis=-1, keepdims=True)
    scale = lax.rsqrt(spread + norm_epsilon)
    return centred * scale, scale


def norm_back(unit, scale, gain, upstream):
    inner = upstream * gain
    mean_inner = jnp.mean(inner, axis=-1, keepdims=True)
    mean_cross = jnp.mean(inner * unit, axis=-1, keepdims=True)
    return scale * (inner - mean_inner - unit * mean_cross)


def after(value, *others):
    return lax.optimization_barrier((value, *others))[0]


class Grid:
    def __init__(self):
        self.size = lax.axis_size("fsdp")
        self.index = lax.axis_index("fsdp")
        self.core = lax.axis_index("dp")
        bits = self.size.bit_length() - 1
        side = bits // 3
        x_bits = tuple(range(side))
        y_bits = tuple(range(side, 2 * side))
        self.orders = (x_bits + y_bits, y_bits + x_bits)
        self.steps = 2 * side
        self.low_bits = tuple(range(2 * side, bits - 1))
        self.top_bit = bits - 1
        self.top = self.index >> self.top_bit

    def swap(self, value, bit):
        return lax.ppermute(value, "fsdp", [(i, i ^ (1 << bit)) for i in range(self.size)])

    def swap_step(self, value, step):
        pairs = []
        for core in range(2):
            bit = self.orders[core][step]
            for i in range(self.size):
                pairs.append((core * self.size + i, core * self.size + (i ^ (1 << bit))))
        return lax.ppermute(value, ("dp", "fsdp"), pairs)

    def swap_core(self, value):
        return lax.ppermute(value, "dp", [(0, 1), (1, 0)])

    def swap_owned(self, value, bit, owned):
        pairs = []
        for core in range(2):
            for i in range(self.size):
                if ((i >> self.top_bit) == core) == owned:
                    pairs.append((core * self.size + i, core * self.size + (i ^ (1 << bit))))
        return lax.ppermute(value, ("dp", "fsdp"), pairs)

    def flip_step(self, rels, step):
        masks = [1 << self.orders[core][step] for core in range(2)]
        return tuple((rel[0] ^ masks[0], rel[1] ^ masks[1]) for rel in rels)


def flip_bit(rels, bit):
    return tuple((rel[0] ^ (1 << bit), rel[1] ^ (1 << bit)) for rel in rels)


class Gather:
    def __init__(self, grid, block, owned):
        self.grid, self.owned = grid, owned
        self.value, self.rels = block[None], ((0, 0),)
        self.done, self.last = [], None

    def high(self):
        grid = self.grid
        if self.owned:
            got = grid.swap_owned(self.value, grid.top_bit, True)
            self.value = jnp.where(grid.top == grid.core, self.value, got)
        else:
            got = grid.swap(self.value, grid.top_bit)
            self.value = jnp.concatenate([self.value, got], axis=0)
            self.rels = self.rels + flip_bit(self.rels, grid.top_bit)

    def low(self, apart):
        grid = self.grid
        self.start = [(self.rels, self.value)]
        for bit in grid.low_bits:
            self.start += [
                (flip_bit(rels, bit), grid.swap(value, bit)) for rels, value in self.start
            ]
        if not apart:
            rels = sum((rels for rels, _ in self.start), ())
            self.start = [(rels, jnp.concatenate([value for _, value in self.start], axis=0))]

    def first(self, which):
        grid = self.grid
        rels, value = self.start[which]
        one = (grid.flip_step(rels, 0), grid.swap_step(value, 0))
        middle = grid.steps // 2
        two = (grid.flip_step(rels, middle), grid.swap_step(value, middle))
        return [(rels, value), one], two

    def second(self, state):
        grid = self.grid
        pieces, early = state
        middle = grid.steps // 2
        for step in range(1, grid.steps):
            new = []
            for place, (rels, value) in enumerate(pieces):
                if step == middle and place == 0:
                    new.append(early)
                else:
                    new.append((grid.flip_step(rels, step), grid.swap_step(value, step)))
            pieces = pieces + new
        return pieces


def pick(rel, core):
    return jnp.where(core == 0, rel[0], rel[1])


def assemble(grid, pieces, count):
    rows, width = pieces[0][1].shape[1:]
    whole = jnp.zeros((count, rows, width), pieces[0][1].dtype)
    for rels, piece in pieces:
        for place, rel in enumerate(rels):
            spot = (grid.index ^ pick(rel, grid.core)) & (count - 1)
            whole = lax.dynamic_update_slice(whole, piece[place : place + 1], (spot, 0, 0))
    return whole.reshape(count * rows, width)


def sum_all(grid, value):
    value = value + grid.swap_core(value)
    for bit in range(grid.top_bit + 1):
        value = value + grid.swap(value, bit)
    return value


def adamw(master, first, second, gradient, rate):
    first_new = beta_one * first + (1.0 - beta_one) * gradient
    second_new = beta_two * second + (1.0 - beta_two) * gradient * gradient
    first_hat = first_new / (1.0 - beta_one**STEP_COUNT)
    second_hat = second_new / (1.0 - beta_two**STEP_COUNT)
    master_new = master - rate * (
        first_hat / (jnp.sqrt(second_hat) + epsilon) + weight_decay * master
    )
    return (master_new, first_new, second_new, master_new.astype(jnp.bfloat16))


RAW, HELD, FETCH, PUT, SCALAR = "raw", "held", "fetch", "put", "scalar"
SPACES = {RAW: pltpu.HBM, HELD: pltpu.VMEM, FETCH: pltpu.HBM, PUT: pltpu.HBM, SCALAR: pltpu.SMEM}


def shaped(shape, dtype):
    return jax.ShapeDtypeStruct(shape, dtype)


class Fetched:
    def __init__(self, copy, room):
        self.copy, self.room, self.waited = copy, room, False

    def ready(self):
        if not self.waited:
            self.copy.wait()
            self.waited = True
        return self.room


def call(body, name, operands, kinds, outs, out_kinds, scratch):
    moved = [o for o, kind in zip(operands, kinds) if kind == FETCH]
    moved += [o for o, kind in zip(outs, out_kinds) if kind == PUT]
    rooms = [pltpu.VMEM(o.shape, o.dtype) for o in moved]
    scratch = list(scratch)

    def whole(*refs):
        ins = refs[: len(operands)]
        results = refs[len(operands) : len(operands) + len(outs)]
        own = refs[len(operands) + len(outs) :]
        own, rest = own[: len(scratch)], own[len(scratch) :]
        room = list(rest[: len(moved)])
        sems = rest[len(moved)] if moved else None
        taken, arrived, written, puts = 0, [], [], []
        for ref, kind in zip(ins, kinds):
            if kind == FETCH:
                copy = pltpu.make_async_copy(ref, room[taken], sems.at[taken])
                copy.start()
                arrived.append(Fetched(copy, room[taken]))
                taken += 1
            else:
                arrived.append(ref)
        for ref, kind in zip(results, out_kinds):
            if kind == PUT:
                puts.append(pltpu.make_async_copy(room[taken], ref, sems.at[taken]))
                written.append(room[taken])
                taken += 1
            else:
                written.append(ref)
        body(*arrived, *written, *own)
        for ref in arrived:
            if isinstance(ref, Fetched):
                ref.ready()
        start_all(puts)
        wait_all(puts)

    return pl.pallas_call(
        whole,
        name=name,
        out_shape=tuple(outs),
        in_specs=[pl.BlockSpec(memory_space=SPACES[kind]) for kind in kinds],
        out_specs=tuple(pl.BlockSpec(memory_space=SPACES[kind]) for kind in out_kinds),
        scratch_shapes=scratch
        + rooms
        + ([pltpu.SemaphoreType.DMA((len(moved),))] if moved else []),
        compiler_params=pltpu.CompilerParams(vmem_limit_bytes=(60 if name == "pack_blocks" else 48) << 20),
        cost_estimate=pl.CostEstimate(flops=int({'pack_blocks': 1.5, 'attend': 4.3, 'grow': 9.5, 'shrink_back': 6.4, 'expand_grads': 4.3, 'attend_back': 8.1, 'joint_back': 2.9, 'finish': 2.6}[name] * 1150000000), bytes_accessed=1, transcendentals=0),
    )(*operands)


class Layout:
    def __init__(self, count, rows, width):
        self.count, self.rows, self.width = count, rows, width
        self.direct = rows % 16 == 0

    def offset(self, index, core, rel):
        if rel[0] == rel[1]:
            spot = (index ^ rel[0]) & (self.count - 1)
        else:
            spot = (index ^ jnp.where(core == 0, rel[0], rel[1])) & (self.count - 1)
        return pl.multiple_of(spot * self.rows, 16)


class Loading:
    def __init__(self, pieces, refs, meta_ref, scratch):
        self.pieces, self.meta = pieces, meta_ref
        self.whole, self.room, self.sems = scratch
        self.copies, at = [], 0
        for place, ref in enumerate(refs):
            target = self.whole
            if pieces.rel_sets is not None:
                target = self.room.at[pl.ds(at, ref.shape[0])]
                at += ref.shape[0]
            self.copies.append(pltpu.make_async_copy(ref, target, self.sems.at[place]))
        start_all(self.copies)

    def ready(self):
        wait_all(self.copies)
        layout = self.pieces.layout
        if self.pieces.rel_sets is not None:
            rels = sum(self.pieces.rel_sets, ())
            for place, rel in enumerate(rels):
                spot = layout.offset(self.meta[0], self.meta[1], rel)
                self.whole[pl.ds(spot, layout.rows)] = self.room[place]
        return self.whole


class Storing:
    def __init__(self, parts, refs, meta_ref, scratch):
        self.parts, self.refs, self.meta = parts, refs, meta_ref
        self.room, self.sems = scratch
        self.copies = []

    def put(self, start, columns, value):
        layout = self.parts.layout
        value = value.astype(half_type)
        if not layout.direct:
            self.room[start : start + value.shape[0], columns] = value
            return
        for at in range(0, value.shape[0], layout.rows):
            place = self.parts.place((start + at) // layout.rows, self.meta)
            self.room[place, :, columns] = value[at : at + layout.rows]

    def send(self):
        if not self.parts.layout.direct:
            self.copies = [pltpu.make_async_copy(self.room, self.refs[0], self.sems.at[0])]
        else:
            quarter = self.parts.layout.count // 4
            starts = (2 * quarter, quarter, 0)
            self.copies = [
                pltpu.make_async_copy(
                    self.room.at[pl.ds(at, ref.shape[0])], ref, self.sems.at[place]
                )
                for place, (ref, at) in enumerate(zip(self.refs, starts))
            ]
        start_all(self.copies)

    def wait(self):
        wait_all(self.copies)


def start_all(copies):
    for copy in copies:
        copy.start()


def wait_all(copies):
    for copy in copies:
        copy.wait()


class Pieces:
    def __init__(self, grid, pieces, count):
        rows, width = pieces[0][1].shape[1:]
        self.layout = Layout(count, rows, width)
        if self.layout.direct:
            self.rel_sets = [rels for rels, _ in pieces]
            self.arrays = [piece for _, piece in pieces]
        else:
            self.rel_sets = None
            self.arrays = [assemble(grid, pieces, count)]

    def scratch(self):
        count, rows, width = self.layout.count, self.layout.rows, self.layout.width
        room = (count, rows, width) if self.rel_sets is not None else (1, 16, 128)
        return [
            pltpu.VMEM((count * rows, width), half_type),
            pltpu.VMEM(room, half_type),
            pltpu.SemaphoreType.DMA((len(self.arrays),)),
        ]


class Parts:
    def __init__(self, grid, layout, lasting):
        self.grid, self.layout = grid, layout
        count = layout.count
        self.bits = bits = [[*grid.orders[core], *lasting] for core in range(2)]
        rels = []
        for place in range(count):
            taken = [(place >> at) & 1 for at in range(len(bits[0]))][::-1]
            rels.append(
                tuple(
                    sum(1 << bit for bit, take in zip(bits[core], taken) if take)
                    for core in range(2)
                )
            )
        self.rels = tuple(rels)
        quarter = count // 4
        self.rel_sets = [rels[2 * quarter :], rels[quarter : 2 * quarter], rels[:quarter]]

    def shapes(self):
        rows, width = self.layout.rows, self.layout.width
        if self.layout.direct:
            return [shaped((len(rels), rows, width), half_type) for rels in self.rel_sets]
        return [shaped((self.layout.count * rows, width), half_type)]

    def scratch(self):
        count, rows, width = self.layout.count, self.layout.rows, self.layout.width
        shape = (count, rows, width) if self.layout.direct else (count * rows, width)
        return [pltpu.VMEM(shape, half_type), pltpu.SemaphoreType.DMA((3,))]

    def place(self, block, meta_ref):
        rel = (meta_ref[0] ^ block) & (self.layout.count - 1)
        spots = []
        for order in self.bits:
            last = len(order) - 1
            spots.append(sum(((rel >> bit) & 1) << (last - at) for at, bit in enumerate(order)))
        return jnp.where(meta_ref[1] == 0, spots[0], spots[1])

    def split_up(self, arrays):
        if self.layout.direct:
            return arrays
        grid, count = self.grid, self.layout.count
        blocks = arrays[0].reshape(count, self.layout.rows, self.layout.width)
        order = jnp.stack([(grid.index ^ pick(rel, grid.core)) & (count - 1) for rel in self.rels])
        blocks = jnp.take(blocks, order, axis=0, mode="clip")
        return blocks[count // 2 :], blocks[count // 4 : count // 2], blocks[: count // 4]

    def first(self, arrays):
        send, next_send, keep = self.split_up(arrays)
        got = self.grid.swap_step(send, 0)
        middle = got.shape[0] // 2
        return join(next_send, got[middle:]), join(keep, got[:middle])

    def second(self, state):
        send, keep = state
        for step in range(1, self.grid.steps):
            got = self.grid.swap_step(send, step)
            if step == self.grid.steps - 1:
                return keep, got
            middle = keep.shape[0] // 2
            send, keep = join(keep[middle:], got[middle:]), join(keep[:middle], got[:middle])


def join(keep, got):
    return (keep.astype(wide) + got.astype(wide)).astype(half_type)


def third_sum(grid, keep, got, owned=False):
    near, far = keep, got
    for bit in grid.low_bits[::-1]:
        middle = near.shape[0] // 2
        send, near = join(near[middle:], far[middle:]), join(near[:middle], far[:middle])
        far = grid.swap(send, bit)
    if owned:
        last = grid.swap_owned(join(near, far), grid.top_bit, False)
    else:
        middle = near.shape[0] // 2
        last = grid.swap(join(near[middle:], far[middle:]), grid.top_bit)
        near, far = near[:middle], far[:middle]
    return (near.astype(wide) + far.astype(wide) + last.astype(wide))[0]


def pack_blocks(meta, lengths, tokens, cot, joint, output, expand, gains, biases):
    rows = joint.shape[0]
    count, width = tokens.shape
    half = width // 2
    hidden = expand.shape[1] // 2
    small = gains.shape[0] + biases.shape[0]

    def body(meta_ref, lengths_ref, tokens_ref, cot_ref, joint_ref, output_ref, expand_ref, gain_ref, bias_ref, one_ref, two_ref, item_ref, room):
        core = meta_ref[1]
        side = pl.multiple_of(core * half, 128)
        gains_count = gain_ref.room.shape[0]
        room[...] = jnp.zeros_like(room)
        room[:gains_count, :rows] = gain_ref.ready()[...].astype(wide)
        room[gains_count:small, :rows] = bias_ref.ready()[...].astype(wide)
        one_ref[:, 4 * half :] = room[...].T[:rows].astype(half_type)
        mat = joint_ref.ready()
        for part in range(3):
            one_ref[:, part * half : (part + 1) * half] = mat[
                :, pl.ds(pl.multiple_of(part * width + side, 128), half)
            ]
        one_ref[:, 3 * half : 4 * half] = output_ref.ready()[:, pl.ds(side, half)]
        two_ref[...] = expand_ref.ready()[:, pl.ds(pl.multiple_of(core * hidden, 128), hidden)]
        line = (16, width)
        lane = lax.broadcasted_iota(jnp.int32, line, 1)
        value = jnp.where(lane == 0, lengths_ref[0], jnp.where(lane == 1, lengths_ref[1], 0))
        item_ref[:count] = tokens_ref.ready()[...]
        item_ref[count : 2 * count] = cot_ref.ready()[...]
        item_ref[2 * count :] = value.astype(wide).astype(half_type)

    return call(
        body,
        "pack_blocks",
        (meta, lengths, tokens, cot, joint, output, expand, gains, biases),
        (SCALAR, SCALAR) + (FETCH,) * 7,
        (
            shaped((rows, 4 * half + 128), half_type),
            shaped((rows, hidden), half_type),
            shaped((2 * count + 16, width), half_type),
        ),
        (PUT, PUT, PUT),
        (pltpu.VMEM((128, 128), wide),),
    )


def lane_is_low(shape):
    return lax.broadcasted_iota(jnp.int32, shape, 1) < HEAD_DIM


def two_heads(value, low):
    zero = jnp.zeros_like(value)
    return jnp.concatenate([jnp.where(low, value, zero), jnp.where(low, zero, value)], axis=0)


def one_of_two(value, low):
    rows = value.shape[0] // 2
    return jnp.where(low, value[:rows], value[rows:])


def attend(meta, lengths, tokens, item_got, joint):
    tokens_rows, width = tokens.shape
    half = width // 2
    rows = 2 * tokens_rows
    pairs = half // 128

    def body(meta_ref, lengths_ref, own_ref, item_ref, *rest):
        pieces = rest[: len(joint.arrays)]
        normed_ref, projected_ref, attention_ref, attended_ref, output_ref, small_ref = rest[
            len(joint.arrays) : len(joint.arrays) + 6
        ]
        core = meta_ref[1]
        loading = Loading(joint, pieces, meta_ref, rest[len(joint.arrays) + 6 :])
        sides = (own_ref.ready()[...], item_ref.ready()[:tokens_rows])
        units = [norm_parts(side.astype(wide))[0] for side in sides]
        mat = loading.ready()
        small_ref[...] = mat[:, 4 * half :].astype(wide).T[:16]
        output_ref[...] = mat[:, 3 * half : 4 * half]
        side = pl.multiple_of(core * half, 128)
        for item in range(2):
            normed_ref[item * tokens_rows : (item + 1) * tokens_rows] = (
                units[item] * small_ref[0:1] + small_ref[2:3]
            ).astype(half_type)
        normed = normed_ref[...]
        for part in range(3):
            spot = slice(part * half, (part + 1) * half)
            value = matmul(normed, mat[:, spot])
            if part != 1:
                row = 4 if part == 0 else 5
                value = value + small_ref[row : row + 1, pl.ds(side, half)]
            projected_ref[:, spot] = value.astype(half_type)
        low = lane_is_low((tokens_rows, 128))
        query = lax.broadcasted_iota(jnp.int32, (rows, tokens_rows), 0) % tokens_rows
        key = lax.broadcasted_iota(jnp.int32, (rows, tokens_rows), 1)
        for item in range(2):
            if item == 0:
                prefix, total = lengths_ref[0], lengths_ref[1]
            else:
                line = item_ref.room[2 * tokens_rows : 2 * tokens_rows + 16].astype(wide)
                prefix = line[0:1, 0:1].astype(jnp.int32)
                total = line[0:1, 1:2].astype(jnp.int32)
            visible = (key < total) & ((key <= query) | (key < prefix))
            take = slice(item * tokens_rows, (item + 1) * tokens_rows)
            for pair in range(pairs):
                spot = slice(pair * 128, (pair + 1) * 128)
                queries = two_heads(projected_ref[take, spot], low)
                keys = projected_ref[take, half + pair * 128 : half + (pair + 1) * 128]
                values = projected_ref[take, 2 * half + pair * 128 : 2 * half + (pair + 1) * 128]
                scores = times_back(queries, keys) * HEAD_DIM ** (-0.5)
                scores = jnp.where(visible, scores, -1e30)
                powers = jnp.exp(scores - jnp.max(scores, axis=-1, keepdims=True))
                attention = powers / jnp.sum(powers, axis=-1, keepdims=True)
                attention_ref[item * pairs + pair] = attention
                mixed = matmul(attention.astype(half_type), values)
                attended_ref[take, spot] = one_of_two(mixed, low).astype(half_type)

    return call(
        body,
        "attend",
        (meta, lengths, tokens, item_got, *joint.arrays),
        (SCALAR, SCALAR, FETCH, FETCH) + (RAW,) * len(joint.arrays),
        (
            shaped((rows, width), half_type),
            shaped((rows, 3 * half), half_type),
            shaped((2 * pairs, rows, tokens_rows), wide),
            shaped((rows, half), half_type),
            shaped((width, half), half_type),
            shaped((16, width), wide),
        ),
        (HELD, HELD, HELD, PUT, PUT, HELD),
        joint.scratch(),
    )


def flipped(ref):
    rows = ref.shape[0] // 2
    return jnp.concatenate([ref[rows:], ref[:rows]], axis=0)


def grow(meta, small, tokens, cot, item_got, attended, attended_got, output, output_got, expand, quarters):
    tokens_rows, width = tokens.shape
    half = width // 2
    rows = 2 * tokens_rows
    hidden = expand.layout.width
    shapes = quarters.shapes()
    step = 384

    def body(meta_ref, small_ref, own_ref, cot_ref, item_ref, attended_ref, attended_got_ref, output_ref, output_got_ref, *rest):
        pieces = rest[: len(expand.arrays)]
        rest = rest[len(expand.arrays) :]
        middle_ref, normed_ref, active_ref, slope_ref, mixed_ref = rest[:5]
        grads = rest[5 : 5 + len(shapes)]
        *scratch, upstream = rest[5 + len(shapes) :]
        core = meta_ref[1]
        loading = Loading(expand, pieces, meta_ref, scratch[:3])
        storing = Storing(quarters, grads, meta_ref, scratch[3:])
        mine = pl.ds(pl.multiple_of(core * half, 128), half)
        yours = pl.ds(pl.multiple_of((1 - core) * half, 128), half)
        mixed_ref[:, mine] = attended_ref.ready()[...]
        mixed_ref[:, yours] = flipped(attended_got_ref.ready())
        mixed = mixed_ref[...]
        middle_ref[:, mine] = matmul(mixed, output_ref.ready()[...])
        middle_ref[:, yours] = matmul(mixed, output_got_ref.ready()[...])
        sides = (own_ref.ready()[...], item_ref.ready()[:tokens_rows])
        for item, side in enumerate(sides):
            take = slice(item * tokens_rows, (item + 1) * tokens_rows)
            middle = side.astype(wide) + (middle_ref[take] + small_ref[6:7])
            middle_ref[take] = middle
            unit, _ = norm_parts(middle)
            normed_ref[take] = (unit * small_ref[1:2] + small_ref[3:4]).astype(half_type)
        upstream[:tokens_rows] = cot_ref.ready()[...]
        upstream[tokens_rows:] = item_ref.ready()[tokens_rows : 2 * tokens_rows]
        mat = loading.ready()
        normed = normed_ref[...]
        back = upstream[...]
        for at in range(0, hidden, step):
            spot = slice(at, at + step)
            row = 8 + core * (hidden // width) + at // width
            bias = small_ref[pl.ds(row, 1), at % width : at % width + step]
            value = matmul(normed, mat[:, spot]) + bias
            square = value * value
            bent = jnp.tanh(curve * (value + cubic * value * square))
            active = (0.5 * value * (1.0 + bent)).astype(half_type)
            active_ref[:, spot] = active
            slope_ref[:, spot] = 0.5 * (1.0 + bent) + 0.5 * value * (1.0 - bent * bent) * (
                curve * (1.0 + 3.0 * cubic * square)
            )
            storing.put(at, slice(None), outer_sum(active, back))
        storing.send()
        storing.wait()

    outs = (
        shaped((rows, width), wide),
        shaped((rows, width), half_type),
        shaped((rows, hidden), half_type),
        shaped((rows, hidden), wide),
        shaped((rows, width), half_type),
    ) + tuple(shapes)
    return call(
        body,
        "grow",
        (meta, small, tokens, cot, item_got, attended, attended_got, output, output_got, *expand.arrays),
        (SCALAR, HELD) + (FETCH,) * 7 + (RAW,) * len(expand.arrays),
        outs,
        (HELD,) * 5 + (RAW,) * len(shapes),
        (*expand.scratch(), *quarters.scratch(), pltpu.VMEM((rows, width), half_type)),
    )


def shrink_back(meta, cot, item_got, slope, shrink, expand):
    tokens_rows, width = cot.shape
    rows = 2 * tokens_rows
    hidden = expand.layout.width

    def body(meta_ref, cot_ref, item_ref, slope_ref, *rest):
        shrink_pieces = rest[: len(shrink.arrays)]
        rest = rest[len(shrink.arrays) :]
        expand_pieces = rest[: len(expand.arrays)]
        hidden_ref, part_ref, *scratch, upstream = rest[len(expand.arrays) :]
        first = Loading(shrink, shrink_pieces, meta_ref, scratch[:3])
        second = Loading(expand, expand_pieces, meta_ref, scratch[3:])
        upstream[:tokens_rows] = cot_ref.ready()[...]
        upstream[tokens_rows:] = item_ref.ready()[tokens_rows : 2 * tokens_rows]
        mat = first.ready()
        step = 384
        for at in range(0, hidden, step):
            spot = slice(at, at + step)
            value = times_back(upstream[...], mat[spot])
            hidden_ref[:, spot] = (value * slope_ref[:, spot]).astype(half_type)
        other = second.ready()
        part_ref[...] = times_back(hidden_ref[...], other[...])

    return call(
        body,
        "shrink_back",
        (meta, cot, item_got, slope, *shrink.arrays, *expand.arrays),
        (SCALAR, FETCH, FETCH, HELD) + (RAW,) * (len(shrink.arrays) + len(expand.arrays)),
        (shaped((rows, hidden), half_type), shaped((rows, width), wide)),
        (HELD, PUT),
        (*shrink.scratch(), *expand.scratch(), pltpu.VMEM((rows, width), half_type)),
    )


def expand_grads(meta, active, normed_two, back_hidden, shrink, quarters):
    rows, hidden = active.shape
    width = normed_two.shape[1]
    tokens_rows = rows // 2
    shapes = quarters.shapes()

    def body(meta_ref, active_ref, normed_ref, hidden_ref, *rest):
        pieces = rest[: len(shrink.arrays)]
        rest = rest[len(shrink.arrays) :]
        own_ref, other_ref, bias_ref = rest[:3]
        grads = rest[3 : 3 + len(shapes)]
        scratch = rest[3 + len(shapes) :]
        loading = Loading(shrink, pieces, meta_ref, scratch[:3])
        storing = Storing(quarters, grads, meta_ref, scratch[3:])
        step = 384
        for at in range(0, hidden, step):
            spot = slice(at, at + step)
            storing.put(0, spot, outer_sum(normed_ref[...], hidden_ref[:, spot]))
        storing.send()
        bias_ref[...] = jnp.sum(hidden_ref[...].astype(wide), axis=0, keepdims=True)
        mat = loading.ready()
        for ref, at in ((own_ref, 0), (other_ref, tokens_rows)):
            ref[...] = matmul(active_ref[at : at + tokens_rows], mat[...])
        storing.wait()

    outs = (
        shaped((tokens_rows, width), wide),
        shaped((tokens_rows, width), wide),
        shaped((1, hidden), wide),
    ) + tuple(shapes)
    return call(
        body,
        "expand_grads",
        (meta, active, normed_two, back_hidden, *shrink.arrays),
        (SCALAR, HELD, HELD, HELD) + (RAW,) * len(shrink.arrays),
        outs,
        (HELD, PUT, HELD) + (RAW,) * len(shapes),
        (*shrink.scratch(), *quarters.scratch()),
    )


def attend_back(meta, small, middle, cot, item_got, part, part_got, mixed, output, output_got, normed, projected, attention, quarters):
    rows, width = middle.shape
    half = width // 2
    tokens_rows = rows // 2
    pairs = half // 128
    shapes = quarters.shapes()

    def body(meta_ref, small_ref, middle_ref, cot_ref, item_ref, part_ref, part_got_ref, mixed_ref, output_ref, output_got_ref, normed_ref, projected_ref, attention_ref, back_middle_ref, back_projected_ref, sums_ref, *rest):
        grads = rest[: len(shapes)]
        *scratch, branch = rest[len(shapes) :]
        core = meta_ref[1]
        storing = Storing(quarters, grads, meta_ref, scratch)
        mine = pl.ds(pl.multiple_of(core * half, 128), half)
        yours = pl.ds(pl.multiple_of((1 - core) * half, 128), half)
        gain = jnp.zeros((1, width), wide)
        shift = jnp.zeros((1, width), wide)
        bias_branch = jnp.zeros((1, width), wide)
        bias_second = jnp.zeros((1, width), wide)
        sides = (cot_ref.ready()[...], item_ref.ready()[tokens_rows : 2 * tokens_rows])
        part_ref, part_got_ref = part_ref.ready(), part_got_ref.ready()
        output_ref, output_got_ref = output_ref.ready(), output_got_ref.ready()
        for item, side in enumerate(sides):
            take = slice(item * tokens_rows, (item + 1) * tokens_rows)
            across = slice((1 - item) * tokens_rows, (2 - item) * tokens_rows)
            unit, scale = norm_parts(middle_ref[take])
            upstream = side.astype(wide)
            back = part_ref[take] + part_got_ref[across].astype(wide)
            value = upstream + norm_back(unit, scale, small_ref[1:2], back)
            if item == 0:
                back_middle_ref[...] = value
            low_value = value.astype(half_type)
            branch[take] = low_value
            gain = gain + jnp.sum(back * unit, axis=0, keepdims=True)
            shift = shift + jnp.sum(back, axis=0, keepdims=True)
            bias_branch = bias_branch + jnp.sum(low_value.astype(wide), axis=0, keepdims=True)
            bias_second = bias_second + jnp.sum(upstream, axis=0, keepdims=True)
        sums_ref[...] = jnp.zeros_like(sums_ref)
        sums_ref[1:2] = 0.5 * gain
        sums_ref[3:4] = 0.5 * shift
        sums_ref[6:7] = 0.5 * bias_branch
        sums_ref[7:8] = 0.5 * bias_second
        storing.put(0, slice(3 * half, 4 * half), outer_sum(mixed_ref[...], branch[:, mine]))
        height = pl.ds(pl.multiple_of(core * half, 128), half)
        back_attended = (
            times_back(branch[:, mine], output_ref[height])
            + times_back(branch[:, yours], output_got_ref[height])
        ).astype(half_type)
        low = lane_is_low((tokens_rows, 128))
        for item in range(2):
            take = slice(item * tokens_rows, (item + 1) * tokens_rows)
            for pair in range(pairs):
                spot = slice(pair * 128, (pair + 1) * 128)
                queries = two_heads(projected_ref[take, spot], low)
                keys = projected_ref[take, half + pair * 128 : half + (pair + 1) * 128]
                values = projected_ref[take, 2 * half + pair * 128 : 2 * half + (pair + 1) * 128]
                upstream = two_heads(back_attended[take, spot], low)
                attention = attention_ref[item * pairs + pair]
                back_values = outer_sum(attention.astype(half_type), upstream)
                back_attention = times_back(upstream, values)
                inner = jnp.sum(attention * back_attention, axis=-1, keepdims=True)
                back_scores = (HEAD_DIM ** (-0.5) * attention * (back_attention - inner)).astype(half_type)
                back_queries = one_of_two(matmul(back_scores, keys), low)
                back_keys = outer_sum(back_scores, queries)
                for part_at, value in enumerate((back_queries, back_keys, back_values)):
                    start = part_at * half + pair * 128
                    back_projected_ref[take, start : start + 128] = value.astype(half_type)
        sums_ref[4:5, mine] = jnp.sum(back_projected_ref[:, :half].astype(wide), axis=0, keepdims=True)
        sums_ref[5:6, mine] = jnp.sum(
            back_projected_ref[:, 2 * half :].astype(wide), axis=0, keepdims=True
        )
        for part_at in range(3):
            spot = slice(part_at * half, (part_at + 1) * half)
            storing.put(0, spot, outer_sum(normed_ref[...], back_projected_ref[:, spot]))
        storing.send()
        storing.wait()

    outs = (
        shaped((tokens_rows, width), wide),
        shaped((rows, 3 * half), half_type),
        shaped((16, width), wide),
    ) + tuple(shapes)
    return call(
        body,
        "attend_back",
        (meta, small, middle, cot, item_got, part, part_got, mixed, output, output_got, normed, projected, attention),
        (SCALAR, HELD, HELD, FETCH, FETCH, FETCH, FETCH, HELD, FETCH, FETCH, HELD, HELD, HELD),
        outs,
        (HELD,) * 3 + (RAW,) * len(shapes),
        (*quarters.scratch(), pltpu.VMEM((rows, width), half_type)),
    )


def joint_back(meta, back_projected, joint, width):
    rows, depth = back_projected.shape
    tokens_rows = rows // 2

    def body(meta_ref, back_ref, *rest):
        pieces = rest[: len(joint.arrays)]
        own_ref, other_ref, *scratch = rest[len(joint.arrays) :]
        mat = Loading(joint, pieces, meta_ref, scratch).ready()
        other_ref[...] = times_back(back_ref[tokens_rows:], mat[:, :depth])
        own_ref[...] = times_back(back_ref[:tokens_rows], mat[:, :depth])

    return call(
        body,
        "joint_back",
        (meta, back_projected, *joint.arrays),
        (SCALAR, HELD) + (RAW,) * len(joint.arrays),
        (shaped((tokens_rows, width), wide), shaped((tokens_rows, width), wide)),
        (HELD, PUT),
        joint.scratch(),
    )


def finish(meta, small, tokens, middle, second, second_got, back_middle, back_one, back_got, sums, expand_bias):
    tokens_rows, width = tokens.shape
    hidden = expand_bias.shape[1]

    def body(meta_ref, small_ref, own_ref, middle_ref, second_ref, second_got_ref, back_middle_ref, back_ref, back_got_ref, sums_ref, bias_ref, result_ref, input_ref, total_ref):
        core = meta_ref[1]
        result_ref[...] = middle_ref[:tokens_rows] + (
            second_ref[...] + second_got_ref.ready()[...] + small_ref[7:8]
        )
        unit, scale = norm_parts(own_ref.ready()[...].astype(wide))
        back = back_ref[...] + back_got_ref.ready()[...]
        input_ref[...] = back_middle_ref[...] + norm_back(unit, scale, small_ref[0:1], back)
        total_ref[...] = sums_ref[...]
        total_ref[0:1] = jnp.sum(back * unit, axis=0, keepdims=True)
        total_ref[2:3] = jnp.sum(back, axis=0, keepdims=True)
        count = hidden // width
        for at in range(count):
            total_ref[pl.ds(8 + core * count + at, 1)] = bias_ref[:, at * width : (at + 1) * width]

    return call(
        body,
        "finish",
        (meta, small, tokens, middle, second, second_got, back_middle, back_one, back_got, sums, expand_bias),
        (SCALAR, HELD, FETCH, HELD, HELD, FETCH, HELD, HELD, FETCH, HELD, HELD),
        (shaped((tokens_rows, width), wide), shaped((tokens_rows, width), wide), shaped((16, width), wide)),
        (PUT, PUT, PUT),
        (),
    )


def local(
    tokens,
    cotangent,
    lengths,
    joint_weight,
    output_weight,
    expand_weight,
    shrink_weight,
    norm_gains,
    bias_rows,
    master_joint,
    master_output,
    master_expand,
    master_shrink,
    master_gains,
    master_biases,
    first_joint,
    first_output,
    first_expand,
    first_shrink,
    first_gains,
    first_biases,
    second_joint,
    second_output,
    second_expand,
    second_shrink,
    second_gains,
    second_biases,
):
    grid = Grid()
    core = grid.core
    size = grid.size
    width = tokens.shape[2]
    half = width // 2
    small_rows = norm_gains.shape[1] + bias_rows.shape[1]
    meta = jnp.stack([grid.index, core])
    lengths_own = lengths[0]
    tokens_own, cot = tokens[0], cotangent[0]
    joint_block, expand_block, item = pack_blocks(
        meta, lengths_own, tokens_own, cot,
        joint_weight[0], output_weight[0], expand_weight[0], norm_gains[0], bias_rows[0],
    )
    item_got = grid.swap_core(item)
    one = Gather(grid, joint_block, False)
    two = Gather(grid, expand_block, False)
    three = Gather(grid, after(shrink_weight[0], joint_block), True)
    one.high()
    two.value = after(two.value, one.value)
    two.high()
    three.value = after(three.value, two.value)
    three.high()
    one.low(True)
    one_near = one.first(0)
    two.value = after(two.value, one_near[0][1][1], one_near[1][1])
    two.low(False)
    three.low(False)
    one.start[1] = (one.start[1][0], after(one.start[1][1], one_near[0][1][1], one_near[1][1]))
    one_far = one.first(1)
    near_pieces = one.second(one_near)
    one_far[0][1] = (one_far[0][1][0], after(one_far[0][1][1], *[piece for _, piece in near_pieces], one_far[1][1]))
    joint = Pieces(grid, near_pieces + one.second(one_far), size)
    two.start[0] = (two.start[0][0], after(two.start[0][1], one_far[0][1][1], one_far[1][1]))
    two_all = two.first(0)
    expand = Pieces(grid, two.second(two_all), size)
    three.start[0] = (three.start[0][0], after(three.start[0][1], two_all[0][1][1]))
    three_all = three.first(0)
    shrink = Pieces(grid, three.second(three_all), size // 2)
    lasting = (*grid.low_bits[::-1], grid.top_bit)
    shrink_quarters = Parts(grid, shrink.layout, lasting[:-1])
    expand_quarters = Parts(grid, expand.layout, lasting)
    joint_quarters = Parts(grid, Layout(size, joint.layout.rows, 4 * half), lasting)

    normed, projected, attention, attended, output, small = attend(
        meta, lengths_own, tokens_own, item_got, joint
    )
    attended_got = after(grid.swap_core(attended), three_all[0][1][1])
    output_got = grid.swap_core(output)
    middle, normed_two, active, slope, mixed, *shrink_grads = grow(
        meta, small, tokens_own, cot, item_got, attended, attended_got,
        output, output_got, expand, shrink_quarters,
    )
    shrink_sum = third_sum(grid, *shrink_quarters.second(shrink_quarters.first(shrink_grads)), owned=True)
    back_hidden, part = shrink_back(meta, cot, item_got, slope, shrink, expand)
    part_got = grid.swap_core(part)
    second, second_other, expand_bias, *expand_grad = expand_grads(
        meta, active, normed_two, back_hidden, shrink, expand_quarters
    )
    expand_sum = third_sum(grid, *expand_quarters.second(expand_quarters.first(expand_grad)))
    second_got = grid.swap_core(second_other)
    back_middle, back_projected, sums, *joint_grad = attend_back(
        meta, small, middle, cot, item_got, part, part_got, mixed, output, output_got,
        normed, projected, attention, joint_quarters,
    )
    joint_first = joint_quarters.first(joint_grad)
    joint_sum_all = third_sum(grid, *joint_quarters.second(joint_first))
    back_one, back_other = joint_back(meta, after(back_projected, joint_first[0]), joint, width)
    back_got = grid.swap_core(back_other)
    result, input_grad, small_grads = finish(
        meta, small, tokens_own, middle, second, second_got, back_middle, back_one, back_got,
        sums, expand_bias,
    )
    small_sum = sum_all(grid, small_grads)
    own = norm_gains.shape[2]
    small_own = lax.dynamic_slice_in_dim(small_sum, grid.index * own, own, axis=1)
    gains_count = norm_gains.shape[1]

    third = [joint_sum_all[:, part_at * half : (part_at + 1) * half] for part_at in range(3)]
    joint_got = grid.swap_core(jnp.where(core == 0, third[2], third[0]))
    joint_sum = jnp.where(
        core == 0,
        jnp.concatenate([third[0], joint_got, third[1]], axis=1),
        jnp.concatenate([third[1], joint_got, third[2]], axis=1),
    )
    output_sum = joint_sum_all[:, 3 * half :]
    owner = grid.top == core
    side = shrink_sum.shape[1] // 2
    shrink_send = lax.dynamic_slice_in_dim(shrink_sum, (1 - core) * side, side, axis=1)
    shrink_keep = lax.dynamic_slice_in_dim(shrink_sum, core * side, side, axis=1)
    shrink_own = jnp.where(owner, shrink_keep, grid.swap_core(shrink_send))

    masters = (
        master_joint,
        master_output,
        master_expand,
        master_shrink,
        master_gains,
        master_biases,
    )
    firsts = (first_joint, first_output, first_expand, first_shrink, first_gains, first_biases)
    seconds = (
        second_joint,
        second_output,
        second_expand,
        second_shrink,
        second_gains,
        second_biases,
    )
    totals_all = (
        joint_sum[None],
        output_sum[None],
        expand_sum[None],
        shrink_own[None],
        small_own[None, :gains_count],
        small_own[None, gains_count:small_rows],
    )
    results = [result[None], input_grad[None]]
    for group_index in range(6):
        group_rate = learning_rate if group_index < 4 else small_rate
        new_master, new_first, new_second, new_copy = adamw(
            masters[group_index],
            firsts[group_index],
            seconds[group_index],
            totals_all[group_index],
            group_rate,
        )
        results.extend([totals_all[group_index], new_master, new_first, new_second, new_copy])
    return tuple(results)


def solution(mesh):
    placed = (
        P(("dp", "fsdp"), None, None),
        P(("dp", "fsdp"), None, None),
        P(("dp", "fsdp"), None),
        P(None, "fsdp", None),
        P(None, "fsdp", None),
        P(None, "fsdp", None),
        P(None, "fsdp", None),
        P(None, None, "fsdp"),
        P(None, None, "fsdp"),
        P(None, "fsdp", "dp"),
        P(None, "fsdp", "dp"),
        P(None, "fsdp", "dp"),
        P(None, "fsdp", "dp"),
        P(None, None, "fsdp"),
        P(None, None, "fsdp"),
        P(None, "fsdp", "dp"),
        P(None, "fsdp", "dp"),
        P(None, "fsdp", "dp"),
        P(None, "fsdp", "dp"),
        P(None, None, "fsdp"),
        P(None, None, "fsdp"),
        P(None, "fsdp", "dp"),
        P(None, "fsdp", "dp"),
        P(None, "fsdp", "dp"),
        P(None, "fsdp", "dp"),
        P(None, None, "fsdp"),
        P(None, None, "fsdp"),
    )
    return jax.shard_map(
        local,
        mesh=mesh,
        in_specs=placed,
        out_specs=(
            P(("dp", "fsdp"), None, None),
            P(("dp", "fsdp"), None, None),
            P(None, "fsdp", "dp"),
            P(None, "fsdp", "dp"),
            P(None, "fsdp", "dp"),
            P(None, "fsdp", "dp"),
            P(None, "fsdp", "dp"),
            P(None, "fsdp", "dp"),
            P(None, "fsdp", "dp"),
            P(None, "fsdp", "dp"),
            P(None, "fsdp", "dp"),
            P(None, "fsdp", "dp"),
            P(None, "fsdp", "dp"),
            P(None, "fsdp", "dp"),
            P(None, "fsdp", "dp"),
            P(None, "fsdp", "dp"),
            P(None, "fsdp", "dp"),
            P(None, "fsdp", "dp"),
            P(None, "fsdp", "dp"),
            P(None, "fsdp", "dp"),
            P(None, "fsdp", "dp"),
            P(None, "fsdp", "dp"),
            P(None, None, "fsdp"),
            P(None, None, "fsdp"),
            P(None, None, "fsdp"),
            P(None, None, "fsdp"),
            P(None, None, "fsdp"),
            P(None, None, "fsdp"),
            P(None, None, "fsdp"),
            P(None, None, "fsdp"),
            P(None, None, "fsdp"),
            P(None, None, "fsdp"),
        ),
        check_vma=False,
    )
```

```python
import jax
import jax.numpy as jnp
from jax import lax
from jax.experimental import pallas as pl
from jax.experimental.pallas import tpu as pltpu
from jax.sharding import PartitionSpec as P

HEAD_DIM = 64
STEP_COUNT = 3


beta_one = 0.5
beta_two = 0.5
learning_rate = 0.02
small_rate = 0.25
weight_decay = 0.1
epsilon = 1e-08
norm_epsilon = 1e-05
curve = 0.7978845608028654
cubic = 0.044715
half_type = jnp.bfloat16
wide = jnp.float32


def matmul(left, right):
    return lax.dot_general(left, right, (((1,), (0,)), ((), ())), preferred_element_type=wide)


def outer_sum(left, right):
    return lax.dot_general(left, right, (((0,), (0,)), ((), ())), preferred_element_type=wide)


def times_back(left, right):
    return lax.dot_general(left, right, (((1,), (1,)), ((), ())), preferred_element_type=wide)


def norm_parts(stream):
    centred = stream - jnp.mean(stream, axis=-1, keepdims=True)
    spread = jnp.mean(centred * centred, axis=-1, keepdims=True)
    scale = lax.rsqrt(spread + norm_epsilon)
    return centred * scale, scale


def norm_back(unit, scale, gain, upstream):
    inner = upstream * gain
    mean_inner = jnp.mean(inner, axis=-1, keepdims=True)
    mean_cross = jnp.mean(inner * unit, axis=-1, keepdims=True)
    return scale * (inner - mean_inner - unit * mean_cross)


def after(value, *others):
    return lax.optimization_barrier((value, *others))[0]


class Grid:
    def __init__(self):
        self.size = lax.axis_size("fsdp")
        self.index = lax.axis_index("fsdp")
        self.core = lax.axis_index("dp")
        bits = self.size.bit_length() - 1
        side = bits // 3
        x_bits = tuple(range(side))
        y_bits = tuple(range(side, 2 * side))
        self.orders = (x_bits + y_bits, y_bits + x_bits)
        self.steps = 2 * side
        self.low_bits = tuple(range(2 * side, bits - 1))
        self.top_bit = bits - 1
        self.top = self.index >> self.top_bit

    def swap(self, value, bit):
        return lax.ppermute(value, "fsdp", [(i, i ^ (1 << bit)) for i in range(self.size)])

    def swap_step(self, value, step):
        pairs = []
        for core in range(2):
            bit = self.orders[core][step]
            for i in range(self.size):
                pairs.append((core * self.size + i, core * self.size + (i ^ (1 << bit))))
        return lax.ppermute(value, ("dp", "fsdp"), pairs)

    def swap_core(self, value):
        return lax.ppermute(value, "dp", [(0, 1), (1, 0)])

    def swap_owned(self, value, bit, owned):
        pairs = []
        for core in range(2):
            for i in range(self.size):
                if ((i >> self.top_bit) == core) == owned:
                    pairs.append((core * self.size + i, core * self.size + (i ^ (1 << bit))))
        return lax.ppermute(value, ("dp", "fsdp"), pairs)

    def flip_step(self, rels, step):
        masks = [1 << self.orders[core][step] for core in range(2)]
        return tuple((rel[0] ^ masks[0], rel[1] ^ masks[1]) for rel in rels)


def flip_bit(rels, bit):
    return tuple((rel[0] ^ (1 << bit), rel[1] ^ (1 << bit)) for rel in rels)


class Gather:
    def __init__(self, grid, block, owned):
        self.grid, self.owned = grid, owned
        self.value, self.rels = block[None], ((0, 0),)
        self.done, self.last = [], None

    def high(self):
        grid = self.grid
        if self.owned:
            got = grid.swap_owned(self.value, grid.top_bit, True)
            self.value = jnp.where(grid.top == grid.core, self.value, got)
        else:
            got = grid.swap(self.value, grid.top_bit)
            self.value = jnp.concatenate([self.value, got], axis=0)
            self.rels = self.rels + flip_bit(self.rels, grid.top_bit)

    def low(self, apart):
        grid = self.grid
        self.start = [(self.rels, self.value)]
        for bit in grid.low_bits:
            self.start += [
                (flip_bit(rels, bit), grid.swap(value, bit)) for rels, value in self.start
            ]
        if not apart:
            rels = sum((rels for rels, _ in self.start), ())
            self.start = [(rels, jnp.concatenate([value for _, value in self.start], axis=0))]

    def first(self, which):
        grid = self.grid
        rels, value = self.start[which]
        one = (grid.flip_step(rels, 0), grid.swap_step(value, 0))
        middle = grid.steps // 2
        two = (grid.flip_step(rels, middle), grid.swap_step(value, middle))
        return [(rels, value), one], two

    def second(self, state):
        grid = self.grid
        pieces, early = state
        middle = grid.steps // 2
        for step in range(1, grid.steps):
            new = []
            for place, (rels, value) in enumerate(pieces):
                if step == middle and place == 0:
                    new.append(early)
                else:
                    new.append((grid.flip_step(rels, step), grid.swap_step(value, step)))
            pieces = pieces + new
        return pieces


def pick(rel, core):
    return jnp.where(core == 0, rel[0], rel[1])


def assemble(grid, pieces, count):
    rows, width = pieces[0][1].shape[1:]
    whole = jnp.zeros((count, rows, width), pieces[0][1].dtype)
    for rels, piece in pieces:
        for place, rel in enumerate(rels):
            spot = (grid.index ^ pick(rel, grid.core)) & (count - 1)
            whole = lax.dynamic_update_slice(whole, piece[place : place + 1], (spot, 0, 0))
    return whole.reshape(count * rows, width)


def adamw(master, first, second, gradient, rate):
    first_new = beta_one * first + (1.0 - beta_one) * gradient
    second_new = beta_two * second + (1.0 - beta_two) * gradient * gradient
    first_hat = first_new / (1.0 - beta_one**STEP_COUNT)
    second_hat = second_new / (1.0 - beta_two**STEP_COUNT)
    master_new = master - rate * (
        first_hat / (jnp.sqrt(second_hat) + epsilon) + weight_decay * master
    )
    return (master_new, first_new, second_new, master_new.astype(jnp.bfloat16))


RAW, HELD, FETCH, PUT, SCALAR = "raw", "held", "fetch", "put", "scalar"
SPACES = {RAW: pl.ANY, HELD: pltpu.VMEM, FETCH: pl.ANY, PUT: pl.ANY, SCALAR: pltpu.SMEM}


def shaped(shape, dtype):
    return jax.ShapeDtypeStruct(shape, dtype)


class Fetched:
    def __init__(self, copy, room):
        self.copy, self.room, self.waited = copy, room, False

    def ready(self):
        if not self.waited:
            self.copy.wait()
            self.waited = True
        return self.room


def call(body, name, operands, kinds, outs, out_kinds, scratch):
    moved = [o for o, kind in zip(operands, kinds) if kind == FETCH]
    moved += [o for o, kind in zip(outs, out_kinds) if kind == PUT]
    rooms = [pltpu.VMEM(o.shape, o.dtype) for o in moved]
    scratch = list(scratch)

    def whole(*refs):
        ins = refs[: len(operands)]
        results = refs[len(operands) : len(operands) + len(outs)]
        own = refs[len(operands) + len(outs) :]
        own, rest = own[: len(scratch)], own[len(scratch) :]
        room = list(rest[: len(moved)])
        sems = rest[len(moved)] if moved else None
        taken, arrived, written, puts = 0, [], [], []
        for ref, kind in zip(ins, kinds):
            if kind == FETCH:
                copy = pltpu.make_async_copy(ref, room[taken], sems.at[taken])
                copy.start()
                arrived.append(Fetched(copy, room[taken]))
                taken += 1
            else:
                arrived.append(ref)
        for ref, kind in zip(results, out_kinds):
            if kind == PUT:
                puts.append(pltpu.make_async_copy(room[taken], ref, sems.at[taken]))
                written.append(room[taken])
                taken += 1
            else:
                written.append(ref)
        body(*arrived, *written, *own)
        for ref in arrived:
            if isinstance(ref, Fetched):
                ref.ready()
        start_all(puts)
        wait_all(puts)

    return pl.pallas_call(
        whole,
        name=name,
        out_shape=tuple(outs),
        in_specs=[pl.BlockSpec(memory_space=SPACES[kind]) for kind in kinds],
        out_specs=tuple(pl.BlockSpec(memory_space=SPACES[kind]) for kind in out_kinds),
        scratch_shapes=scratch
        + rooms
        + ([pltpu.SemaphoreType.DMA((len(moved),))] if moved else []),
        compiler_params=pltpu.CompilerParams(vmem_limit_bytes=(60 if name == "pack_blocks" else 28) << 20),
        cost_estimate=pl.CostEstimate(flops=int({'pack_blocks': 1.5, 'attend': 4.3, 'grow': 9.5, 'shrink_back': 6.4, 'expand_grads': 4.3, 'attend_back': 9.0, 'finish': 2.6}[name] * 1150000000), bytes_accessed=1, transcendentals=0),
    )(*operands)


class Layout:
    def __init__(self, count, rows, width):
        self.count, self.rows, self.width = count, rows, width
        self.direct = rows % 16 == 0

    def offset(self, index, core, rel):
        if rel[0] == rel[1]:
            spot = (index ^ rel[0]) & (self.count - 1)
        else:
            spot = (index ^ jnp.where(core == 0, rel[0], rel[1])) & (self.count - 1)
        return pl.multiple_of(spot * self.rows, 16)


class Loading:
    def __init__(self, pieces, refs, meta_ref, scratch):
        self.pieces, self.meta = pieces, meta_ref
        self.whole, self.room, self.sems = scratch
        self.copies, at = [], 0
        for place, ref in enumerate(refs):
            target = self.whole
            if pieces.rel_sets is not None:
                target = self.room.at[pl.ds(at, ref.shape[0])]
                at += ref.shape[0]
            self.copies.append(pltpu.make_async_copy(ref, target, self.sems.at[place]))
        start_all(self.copies)

    def ready(self):
        wait_all(self.copies)
        layout = self.pieces.layout
        if self.pieces.rel_sets is not None:
            rels = sum(self.pieces.rel_sets, ())
            for place, rel in enumerate(rels):
                spot = layout.offset(self.meta[0], self.meta[1], rel)
                self.whole[pl.ds(spot, layout.rows)] = self.room[place]
        return self.whole


class Storing:
    def __init__(self, parts, refs, meta_ref, scratch):
        self.parts, self.refs, self.meta = parts, refs, meta_ref
        self.room, self.sems = scratch
        self.copies = []

    def put(self, start, columns, value):
        layout = self.parts.layout
        value = value.astype(half_type)
        if not layout.direct:
            self.room[start : start + value.shape[0], columns] = value
            return
        for at in range(0, value.shape[0], layout.rows):
            place = self.parts.place((start + at) // layout.rows, self.meta)
            self.room[place, :, columns] = value[at : at + layout.rows]

    def send(self):
        if not self.parts.layout.direct:
            self.copies = [pltpu.make_async_copy(self.room, self.refs[0], self.sems.at[0])]
        else:
            quarter = self.parts.layout.count // 4
            starts = (2 * quarter, quarter, 0)
            self.copies = [
                pltpu.make_async_copy(
                    self.room.at[pl.ds(at, ref.shape[0])], ref, self.sems.at[place]
                )
                for place, (ref, at) in enumerate(zip(self.refs, starts))
            ]
        start_all(self.copies)

    def wait(self):
        wait_all(self.copies)


def start_all(copies):
    for copy in copies:
        copy.start()


def wait_all(copies):
    for copy in copies:
        copy.wait()


class Pieces:
    def __init__(self, grid, pieces, count):
        rows, width = pieces[0][1].shape[1:]
        self.layout = Layout(count, rows, width)
        if self.layout.direct:
            self.rel_sets = [rels for rels, _ in pieces]
            self.arrays = [piece for _, piece in pieces]
        else:
            self.rel_sets = None
            self.arrays = [assemble(grid, pieces, count)]

    def scratch(self):
        count, rows, width = self.layout.count, self.layout.rows, self.layout.width
        room = (count, rows, width) if self.rel_sets is not None else (1, 16, 128)
        return [
            pltpu.VMEM((count * rows, width), half_type),
            pltpu.VMEM(room, half_type),
            pltpu.SemaphoreType.DMA((len(self.arrays),)),
        ]


class Parts:
    def __init__(self, grid, layout, lasting):
        self.grid, self.layout = grid, layout
        count = layout.count
        self.bits = bits = [[*grid.orders[core], *lasting] for core in range(2)]
        rels = []
        for place in range(count):
            taken = [(place >> at) & 1 for at in range(len(bits[0]))][::-1]
            rels.append(
                tuple(
                    sum(1 << bit for bit, take in zip(bits[core], taken) if take)
                    for core in range(2)
                )
            )
        self.rels = tuple(rels)
        quarter = count // 4
        self.rel_sets = [rels[2 * quarter :], rels[quarter : 2 * quarter], rels[:quarter]]

    def shapes(self):
        rows, width = self.layout.rows, self.layout.width
        if self.layout.direct:
            return [shaped((len(rels), rows, width), half_type) for rels in self.rel_sets]
        return [shaped((self.layout.count * rows, width), half_type)]

    def scratch(self):
        count, rows, width = self.layout.count, self.layout.rows, self.layout.width
        shape = (count, rows, width) if self.layout.direct else (count * rows, width)
        return [pltpu.VMEM(shape, half_type), pltpu.SemaphoreType.DMA((3,))]

    def place(self, block, meta_ref):
        rel = (meta_ref[0] ^ block) & (self.layout.count - 1)
        spots = []
        for order in self.bits:
            last = len(order) - 1
            spots.append(sum(((rel >> bit) & 1) << (last - at) for at, bit in enumerate(order)))
        return jnp.where(meta_ref[1] == 0, spots[0], spots[1])

    def split_up(self, arrays):
        if self.layout.direct:
            return arrays
        grid, count = self.grid, self.layout.count
        blocks = arrays[0].reshape(count, self.layout.rows, self.layout.width)
        order = jnp.stack([(grid.index ^ pick(rel, grid.core)) & (count - 1) for rel in self.rels])
        blocks = jnp.take(blocks, order, axis=0, mode="clip")
        return blocks[count // 2 :], blocks[count // 4 : count // 2], blocks[: count // 4]

    def first(self, arrays):
        send, next_send, keep = self.split_up(arrays)
        got = self.grid.swap_step(send, 0)
        middle = got.shape[0] // 2
        return join(next_send, got[middle:]), join(keep, got[:middle])

    def second(self, state):
        send, keep = state
        for step in range(1, self.grid.steps):
            got = self.grid.swap_step(send, step)
            if step == self.grid.steps - 1:
                return keep, got
            middle = keep.shape[0] // 2
            send, keep = join(keep[middle:], got[middle:]), join(keep[:middle], got[:middle])


def join(keep, got):
    return (keep.astype(wide) + got.astype(wide)).astype(half_type)


def third_sum(grid, keep, got, owned=False):
    near, far = keep, got
    for bit in grid.low_bits[::-1]:
        middle = near.shape[0] // 2
        send, near = join(near[middle:], far[middle:]), join(near[:middle], far[:middle])
        far = grid.swap(send, bit)
    if owned:
        last = grid.swap_owned(join(near, far), grid.top_bit, False)
    else:
        middle = near.shape[0] // 2
        last = grid.swap(join(near[middle:], far[middle:]), grid.top_bit)
        near, far = near[:middle], far[:middle]
    return (near.astype(wide) + far.astype(wide) + last.astype(wide))[0]


def pack_blocks(meta, lengths, tokens, cot, joint, output, expand, gains, biases):
    rows = joint.shape[0]
    count, width = tokens.shape
    half = width // 2
    hidden = expand.shape[1] // 2
    small = gains.shape[0] + biases.shape[0]

    def body(meta_ref, lengths_ref, tokens_ref, cot_ref, joint_ref, output_ref, expand_ref, gain_ref, bias_ref, one_ref, two_ref, item_ref, room):
        core = meta_ref[1]
        side = pl.multiple_of(core * half, 128)
        gains_count = gain_ref.room.shape[0]
        room[...] = jnp.zeros_like(room)
        room[:gains_count, :rows] = gain_ref.ready()[...].astype(wide)
        room[gains_count:small, :rows] = bias_ref.ready()[...].astype(wide)
        one_ref[:, 4 * half :] = room[...].T[:rows].astype(half_type)
        mat = joint_ref.ready()
        for part in range(3):
            one_ref[:, part * half : (part + 1) * half] = mat[
                :, pl.ds(pl.multiple_of(part * width + side, 128), half)
            ]
        one_ref[:, 3 * half : 4 * half] = output_ref.ready()[:, pl.ds(side, half)]
        two_ref[...] = expand_ref.ready()[:, pl.ds(pl.multiple_of(core * hidden, 128), hidden)]
        line = (16, width)
        lane = lax.broadcasted_iota(jnp.int32, line, 1)
        value = jnp.where(lane == 0, lengths_ref[0], jnp.where(lane == 1, lengths_ref[1], 0))
        item_ref[:count] = tokens_ref.ready()[...]
        item_ref[count : 2 * count] = cot_ref.ready()[...]
        item_ref[2 * count :] = value.astype(wide).astype(half_type)

    return call(
        body,
        "pack_blocks",
        (meta, lengths, tokens, cot, joint, output, expand, gains, biases),
        (SCALAR, SCALAR) + (FETCH,) * 7,
        (
            shaped((rows, 4 * half + 128), half_type),
            shaped((rows, hidden), half_type),
            shaped((2 * count + 16, width), half_type),
        ),
        (PUT, PUT, PUT),
        (pltpu.VMEM((128, 128), wide),),
    )


def lane_is_low(shape):
    return lax.broadcasted_iota(jnp.int32, shape, 1) < HEAD_DIM


def two_heads(value, low):
    zero = jnp.zeros_like(value)
    return jnp.concatenate([jnp.where(low, value, zero), jnp.where(low, zero, value)], axis=0)


def one_of_two(value, low):
    rows = value.shape[0] // 2
    return jnp.where(low, value[:rows], value[rows:])


def attend(meta, lengths, tokens, item_got, joint):
    tokens_rows, width = tokens.shape
    half = width // 2
    rows = 2 * tokens_rows
    pairs = half // 128

    def body(meta_ref, lengths_ref, own_ref, item_ref, *rest):
        pieces = rest[: len(joint.arrays)]
        normed_ref, projected_ref, attention_ref, attended_ref, output_ref, small_ref = rest[
            len(joint.arrays) : len(joint.arrays) + 6
        ]
        core = meta_ref[1]
        loading = Loading(joint, pieces, meta_ref, rest[len(joint.arrays) + 6 :])
        sides = (own_ref.ready()[...], item_ref.ready()[:tokens_rows])
        units = [norm_parts(side.astype(wide))[0] for side in sides]
        mat = loading.ready()
        small_ref[...] = mat[:, 4 * half :].astype(wide).T[:16]
        output_ref[...] = mat[:, 3 * half : 4 * half]
        side = pl.multiple_of(core * half, 128)
        for item in range(2):
            normed_ref[item * tokens_rows : (item + 1) * tokens_rows] = (
                units[item] * small_ref[0:1] + small_ref[2:3]
            ).astype(half_type)
        normed = normed_ref[...]
        for part in range(3):
            spot = slice(part * half, (part + 1) * half)
            value = matmul(normed, mat[:, spot])
            if part != 1:
                row = 4 if part == 0 else 5
                value = value + small_ref[row : row + 1, pl.ds(side, half)]
            projected_ref[:, spot] = value.astype(half_type)
        low = lane_is_low((tokens_rows, 128))
        query = lax.broadcasted_iota(jnp.int32, (rows, tokens_rows), 0) % tokens_rows
        key = lax.broadcasted_iota(jnp.int32, (rows, tokens_rows), 1)
        for item in range(2):
            if item == 0:
                prefix, total = lengths_ref[0], lengths_ref[1]
            else:
                line = item_ref.room[2 * tokens_rows : 2 * tokens_rows + 16].astype(wide)
                prefix = line[0:1, 0:1].astype(jnp.int32)
                total = line[0:1, 1:2].astype(jnp.int32)
            visible = (key < total) & ((key <= query) | (key < prefix))
            take = slice(item * tokens_rows, (item + 1) * tokens_rows)
            for pair in range(pairs):
                spot = slice(pair * 128, (pair + 1) * 128)
                queries = two_heads(projected_ref[take, spot], low)
                keys = projected_ref[take, half + pair * 128 : half + (pair + 1) * 128]
                values = projected_ref[take, 2 * half + pair * 128 : 2 * half + (pair + 1) * 128]
                scores = times_back(queries, keys) * HEAD_DIM ** (-0.5)
                scores = jnp.where(visible, scores, -1e30)
                powers = jnp.exp(scores - jnp.max(scores, axis=-1, keepdims=True))
                attention = powers / jnp.sum(powers, axis=-1, keepdims=True)
                attention_ref[item * pairs + pair] = attention
                mixed = matmul(attention.astype(half_type), values)
                attended_ref[take, spot] = one_of_two(mixed, low).astype(half_type)

    return call(
        body,
        "attend",
        (meta, lengths, tokens, item_got, *joint.arrays),
        (SCALAR, SCALAR, FETCH, FETCH) + (RAW,) * len(joint.arrays),
        (
            shaped((rows, width), half_type),
            shaped((rows, 3 * half), half_type),
            shaped((2 * pairs, rows, tokens_rows), wide),
            shaped((rows, half), half_type),
            shaped((width, half), half_type),
            shaped((16, width), wide),
        ),
        (HELD, HELD, HELD, PUT, PUT, HELD),
        joint.scratch(),
    )


def flipped(ref):
    rows = ref.shape[0] // 2
    return jnp.concatenate([ref[rows:], ref[:rows]], axis=0)


def grow(meta, small, tokens, cot, item_got, attended, attended_got, output, output_got, expand, quarters):
    tokens_rows, width = tokens.shape
    half = width // 2
    rows = 2 * tokens_rows
    hidden = expand.layout.width
    shapes = quarters.shapes()
    step = 384

    def body(meta_ref, small_ref, own_ref, cot_ref, item_ref, attended_ref, attended_got_ref, output_ref, output_got_ref, *rest):
        pieces = rest[: len(expand.arrays)]
        rest = rest[len(expand.arrays) :]
        middle_ref, normed_ref, active_ref, slope_ref, mixed_ref = rest[:5]
        grads = rest[5 : 5 + len(shapes)]
        *scratch, upstream = rest[5 + len(shapes) :]
        core = meta_ref[1]
        loading = Loading(expand, pieces, meta_ref, scratch[:3])
        storing = Storing(quarters, grads, meta_ref, scratch[3:])
        mine = pl.ds(pl.multiple_of(core * half, 128), half)
        yours = pl.ds(pl.multiple_of((1 - core) * half, 128), half)
        mixed_ref[:, mine] = attended_ref.ready()[...]
        mixed_ref[:, yours] = flipped(attended_got_ref.ready())
        mixed = mixed_ref[...]
        middle_ref[:, mine] = matmul(mixed, output_ref.ready()[...])
        middle_ref[:, yours] = matmul(mixed, output_got_ref.ready()[...])
        sides = (own_ref.ready()[...], item_ref.ready()[:tokens_rows])
        for item, side in enumerate(sides):
            take = slice(item * tokens_rows, (item + 1) * tokens_rows)
            middle = side.astype(wide) + (middle_ref[take] + small_ref[6:7])
            middle_ref[take] = middle
            unit, _ = norm_parts(middle)
            normed_ref[take] = (unit * small_ref[1:2] + small_ref[3:4]).astype(half_type)
        upstream[:tokens_rows] = cot_ref.ready()[...]
        upstream[tokens_rows:] = item_ref.ready()[tokens_rows : 2 * tokens_rows]
        mat = loading.ready()
        normed = normed_ref[...]
        back = upstream[...]
        for at in range(0, hidden, step):
            spot = slice(at, at + step)
            row = 8 + core * (hidden // width) + at // width
            bias = small_ref[pl.ds(row, 1), at % width : at % width + step]
            value = matmul(normed, mat[:, spot]) + bias
            square = value * value
            bent = jnp.tanh(curve * (value + cubic * value * square))
            active = (0.5 * value * (1.0 + bent)).astype(half_type)
            active_ref[:, spot] = active
            slope_ref[:, spot] = 0.5 * (1.0 + bent) + 0.5 * value * (1.0 - bent * bent) * (
                curve * (1.0 + 3.0 * cubic * square)
            )
            storing.put(at, slice(None), outer_sum(active, back))
        storing.send()
        storing.wait()

    outs = (
        shaped((rows, width), wide),
        shaped((rows, width), half_type),
        shaped((rows, hidden), half_type),
        shaped((rows, hidden), wide),
        shaped((rows, width), half_type),
    ) + tuple(shapes)
    return call(
        body,
        "grow",
        (meta, small, tokens, cot, item_got, attended, attended_got, output, output_got, *expand.arrays),
        (SCALAR, HELD) + (FETCH,) * 7 + (RAW,) * len(expand.arrays),
        outs,
        (HELD,) * 5 + (RAW,) * len(shapes),
        (*expand.scratch(), *quarters.scratch(), pltpu.VMEM((rows, width), half_type)),
    )


def shrink_back(meta, cot, item_got, slope, active, shrink, expand):
    tokens_rows, width = cot.shape
    rows = 2 * tokens_rows
    hidden = expand.layout.width

    def body(meta_ref, cot_ref, item_ref, slope_ref, active_ref, *rest):
        shrink_pieces = rest[: len(shrink.arrays)]
        rest = rest[len(shrink.arrays) :]
        expand_pieces = rest[: len(expand.arrays)]
        hidden_ref, part_ref, second_ref, other_ref, *scratch, upstream = rest[len(expand.arrays) :]
        first = Loading(shrink, shrink_pieces, meta_ref, scratch[:3])
        second = Loading(expand, expand_pieces, meta_ref, scratch[3:])
        upstream[:tokens_rows] = cot_ref.ready()[...]
        upstream[tokens_rows:] = item_ref.ready()[tokens_rows : 2 * tokens_rows]
        mat = first.ready()
        step = 384
        for at in range(0, hidden, step):
            spot = slice(at, at + step)
            value = times_back(upstream[...], mat[spot])
            hidden_ref[:, spot] = (value * slope_ref[:, spot]).astype(half_type)
        for ref, at in ((second_ref, 0), (other_ref, tokens_rows)):
            ref[...] = matmul(active_ref[at : at + tokens_rows], mat[...])
        other = second.ready()
        part_ref[...] = times_back(hidden_ref[...], other[...])

    return call(
        body,
        "shrink_back",
        (meta, cot, item_got, slope, active, *shrink.arrays, *expand.arrays),
        (SCALAR, FETCH, FETCH, HELD, HELD) + (RAW,) * (len(shrink.arrays) + len(expand.arrays)),
        (
            shaped((rows, hidden), half_type),
            shaped((rows, width), wide),
            shaped((tokens_rows, width), wide),
            shaped((tokens_rows, width), wide),
        ),
        (HELD, PUT, HELD, PUT),
        (*shrink.scratch(), *expand.scratch(), pltpu.VMEM((rows, width), half_type)),
    )


def expand_grads(meta, normed_two, back_hidden, quarters):
    width = normed_two.shape[1]
    hidden = back_hidden.shape[1]
    shapes = quarters.shapes()

    def body(meta_ref, normed_ref, hidden_ref, bias_ref, *rest):
        storing = Storing(quarters, rest[: len(shapes)], meta_ref, rest[len(shapes) :])
        step = 384
        for at in range(0, hidden, step):
            spot = slice(at, at + step)
            storing.put(0, spot, outer_sum(normed_ref[...], hidden_ref[:, spot]))
        storing.send()
        bias_ref[...] = jnp.sum(hidden_ref[...].astype(wide), axis=0, keepdims=True)
        storing.wait()

    return call(
        body,
        "expand_grads",
        (meta, normed_two, back_hidden),
        (SCALAR, HELD, HELD),
        (shaped((1, hidden), wide),) + tuple(shapes),
        (HELD,) + (RAW,) * len(shapes),
        quarters.scratch(),
    )


def attend_back(meta, small, middle, tokens, cot, item_got, part, part_got, mixed, output, output_got, normed, projected, attention, expand_bias, joint, quarters):
    rows, width = middle.shape
    half = width // 2
    tokens_rows = rows // 2
    pairs = half // 128
    shapes = quarters.shapes()

    def body(meta_ref, small_ref, middle_ref, tokens_ref, cot_ref, item_ref, part_ref, part_got_ref, mixed_ref, output_ref, output_got_ref, normed_ref, projected_ref, attention_ref, bias_ref, *rest):
        pieces = rest[: len(joint.arrays)]
        rest = rest[len(joint.arrays) :]
        back_middle_ref, own_ref, other_ref = rest[:3]
        grads = rest[3 : 3 + len(shapes)]
        *scratch, branch, back_projected_ref, sums_ref = rest[3 + len(shapes) :]
        core = meta_ref[1]
        loading = Loading(joint, pieces, meta_ref, scratch[:3])
        storing = Storing(quarters, grads, meta_ref, scratch[3:])
        mine = pl.ds(pl.multiple_of(core * half, 128), half)
        yours = pl.ds(pl.multiple_of((1 - core) * half, 128), half)
        gain = jnp.zeros((1, width), wide)
        shift = jnp.zeros((1, width), wide)
        bias_branch = jnp.zeros((1, width), wide)
        bias_second = jnp.zeros((1, width), wide)
        sides = (cot_ref.ready()[...], item_ref.ready()[tokens_rows : 2 * tokens_rows])
        part_ref, part_got_ref = part_ref.ready(), part_got_ref.ready()
        output_ref, output_got_ref = output_ref.ready(), output_got_ref.ready()
        for item, side in enumerate(sides):
            take = slice(item * tokens_rows, (item + 1) * tokens_rows)
            across = slice((1 - item) * tokens_rows, (2 - item) * tokens_rows)
            unit, scale = norm_parts(middle_ref[take])
            upstream = side.astype(wide)
            back = part_ref[take] + part_got_ref[across].astype(wide)
            value = upstream + norm_back(unit, scale, small_ref[1:2], back)
            if item == 0:
                back_middle_ref[...] = value
            low_value = value.astype(half_type)
            branch[take] = low_value
            gain = gain + jnp.sum(back * unit, axis=0, keepdims=True)
            shift = shift + jnp.sum(back, axis=0, keepdims=True)
            bias_branch = bias_branch + jnp.sum(low_value.astype(wide), axis=0, keepdims=True)
            bias_second = bias_second + jnp.sum(upstream, axis=0, keepdims=True)
        sums_ref[...] = jnp.zeros_like(sums_ref)
        sums_ref[1:2] = 0.5 * gain
        sums_ref[3:4] = 0.5 * shift
        sums_ref[6:7] = 0.5 * bias_branch
        sums_ref[7:8] = 0.5 * bias_second
        storing.put(0, slice(3 * half, 4 * half), outer_sum(mixed_ref[...], branch[:, mine]))
        height = pl.ds(pl.multiple_of(core * half, 128), half)
        back_attended = (
            times_back(branch[:, mine], output_ref[height])
            + times_back(branch[:, yours], output_got_ref[height])
        ).astype(half_type)
        low = lane_is_low((tokens_rows, 128))
        for item in range(2):
            take = slice(item * tokens_rows, (item + 1) * tokens_rows)
            for pair in range(pairs):
                spot = slice(pair * 128, (pair + 1) * 128)
                queries = two_heads(projected_ref[take, spot], low)
                keys = projected_ref[take, half + pair * 128 : half + (pair + 1) * 128]
                values = projected_ref[take, 2 * half + pair * 128 : 2 * half + (pair + 1) * 128]
                upstream = two_heads(back_attended[take, spot], low)
                attention = attention_ref[item * pairs + pair]
                back_values = outer_sum(attention.astype(half_type), upstream)
                back_attention = times_back(upstream, values)
                inner = jnp.sum(attention * back_attention, axis=-1, keepdims=True)
                back_scores = (HEAD_DIM ** (-0.5) * attention * (back_attention - inner)).astype(half_type)
                back_queries = one_of_two(matmul(back_scores, keys), low)
                back_keys = outer_sum(back_scores, queries)
                for part_at, value in enumerate((back_queries, back_keys, back_values)):
                    start = part_at * half + pair * 128
                    back_projected_ref[take, start : start + 128] = value.astype(half_type)
        sums_ref[4:5, mine] = jnp.sum(back_projected_ref[:, :half].astype(wide), axis=0, keepdims=True)
        sums_ref[5:6, mine] = jnp.sum(
            back_projected_ref[:, 2 * half :].astype(wide), axis=0, keepdims=True
        )
        for part_at in range(3):
            spot = slice(part_at * half, (part_at + 1) * half)
            storing.put(0, spot, outer_sum(normed_ref[...], back_projected_ref[:, spot]))
        mat = loading.ready()
        gain = jnp.zeros((1, width), wide)
        shift = jnp.zeros((1, width), wide)
        sides = (tokens_ref.ready()[...], item_ref.ready()[:tokens_rows])
        for item, (side, ref) in enumerate(zip(sides, (own_ref, other_ref))):
            take = slice(item * tokens_rows, (item + 1) * tokens_rows)
            back = times_back(back_projected_ref[take], mat[:, : 3 * half])
            ref[...] = back
            unit, _ = norm_parts(side.astype(wide))
            gain = gain + jnp.sum(back * unit, axis=0, keepdims=True)
            shift = shift + jnp.sum(back, axis=0, keepdims=True)
        sums_ref[0:1] = gain
        sums_ref[2:3] = shift
        count = bias_ref.shape[1] // width
        for at in range(count):
            sums_ref[pl.ds(8 + core * count + at, 1)] = bias_ref[:, at * width : (at + 1) * width]
        storing.put(0, slice(4 * half, 4 * half + 128), sums_ref[...].T)
        storing.send()
        storing.wait()

    outs = (
        shaped((tokens_rows, width), wide),
        shaped((tokens_rows, width), wide),
        shaped((tokens_rows, width), wide),
    ) + tuple(shapes)
    return call(
        body,
        "attend_back",
        (meta, small, middle, tokens, cot, item_got, part, part_got, mixed, output, output_got, normed, projected, attention, expand_bias, *joint.arrays),
        (SCALAR, HELD, HELD, FETCH, FETCH, FETCH, FETCH, FETCH, HELD, FETCH, FETCH, HELD, HELD, HELD, HELD) + (RAW,) * len(joint.arrays),
        outs,
        (HELD, HELD, PUT) + (RAW,) * len(shapes),
        (
            *joint.scratch(),
            *quarters.scratch(),
            pltpu.VMEM((rows, width), half_type),
            pltpu.VMEM((rows, 3 * half), half_type),
            pltpu.VMEM((128, width), wide),
        ),
    )


def finish(meta, small, tokens, middle, second, second_got, back_middle, back_one, back_got):
    tokens_rows, width = tokens.shape

    def body(meta_ref, small_ref, own_ref, middle_ref, second_ref, second_got_ref, back_middle_ref, back_ref, back_got_ref, result_ref, input_ref):
        result_ref[...] = middle_ref[:tokens_rows] + (
            second_ref[...] + second_got_ref.ready()[...] + small_ref[7:8]
        )
        unit, scale = norm_parts(own_ref.ready()[...].astype(wide))
        back = back_ref[...] + back_got_ref.ready()[...]
        input_ref[...] = back_middle_ref[...] + norm_back(unit, scale, small_ref[0:1], back)

    return call(
        body,
        "finish",
        (meta, small, tokens, middle, second, second_got, back_middle, back_one, back_got),
        (SCALAR, HELD, FETCH, HELD, HELD, FETCH, HELD, HELD, FETCH),
        (shaped((tokens_rows, width), wide), shaped((tokens_rows, width), wide)),
        (PUT, PUT),
        (),
    )


def local(
    tokens,
    cotangent,
    lengths,
    joint_weight,
    output_weight,
    expand_weight,
    shrink_weight,
    norm_gains,
    bias_rows,
    master_joint,
    master_output,
    master_expand,
    master_shrink,
    master_gains,
    master_biases,
    first_joint,
    first_output,
    first_expand,
    first_shrink,
    first_gains,
    first_biases,
    second_joint,
    second_output,
    second_expand,
    second_shrink,
    second_gains,
    second_biases,
):
    grid = Grid()
    core = grid.core
    size = grid.size
    width = tokens.shape[2]
    half = width // 2
    small_rows = norm_gains.shape[1] + bias_rows.shape[1]
    meta = jnp.stack([grid.index, core])
    lengths_own = lengths[0]
    tokens_own, cot = tokens[0], cotangent[0]
    joint_block, expand_block, item = pack_blocks(
        meta, lengths_own, tokens_own, cot,
        joint_weight[0], output_weight[0], expand_weight[0], norm_gains[0], bias_rows[0],
    )
    item_got = grid.swap_core(item)
    one = Gather(grid, joint_block, False)
    two = Gather(grid, expand_block, False)
    three = Gather(grid, after(shrink_weight[0], joint_block), True)
    one.high()
    two.value = after(two.value, one.value)
    two.high()
    three.value = after(three.value, two.value)
    three.high()
    one.low(True)
    one_near = one.first(0)
    two.value = after(two.value, one_near[0][1][1], one_near[1][1], one.start[1][1])
    two.low(False)
    three.low(False)
    one.start[1] = (one.start[1][0], after(one.start[1][1], one_near[0][1][1], one_near[1][1]))
    one_far = one.first(1)
    near_pieces = one.second(one_near)
    one_far[0][1] = (one_far[0][1][0], after(one_far[0][1][1], *[piece for _, piece in near_pieces], one_far[1][1]))
    joint = Pieces(grid, near_pieces + one.second(one_far), size)
    two.start[0] = (two.start[0][0], after(two.start[0][1], one_far[0][1][1], one_far[1][1]))
    two_all = two.first(0)
    expand = Pieces(grid, two.second(two_all), size)
    three.start[0] = (three.start[0][0], after(three.start[0][1], two_all[0][1][1]))
    three_all = three.first(0)
    shrink = Pieces(grid, three.second(three_all), size // 2)
    lasting = (*grid.low_bits[::-1], grid.top_bit)
    shrink_quarters = Parts(grid, shrink.layout, lasting[:-1])
    expand_quarters = Parts(grid, expand.layout, lasting)
    joint_quarters = Parts(grid, Layout(size, joint.layout.rows, 4 * half + 128), lasting)

    normed, projected, attention, attended, output, small = attend(
        meta, lengths_own, tokens_own, item_got, joint
    )
    attended_got = after(
        grid.swap_core(after(attended, expand.arrays[-1])), three_all[0][1][1], three_all[1][1]
    )
    output_got = grid.swap_core(output)
    middle, normed_two, active, slope, mixed, *shrink_grads = grow(
        meta, small, tokens_own, cot, item_got, attended, attended_got,
        output, output_got, expand, shrink_quarters,
    )
    shrink_sum = third_sum(grid, *shrink_quarters.second(shrink_quarters.first(shrink_grads)), owned=True)
    back_hidden, part, second, second_other = shrink_back(
        meta, cot, item_got, slope, active, shrink, expand
    )
    part_got = grid.swap_core(part)
    expand_bias, *expand_grad = expand_grads(meta, normed_two, back_hidden, expand_quarters)
    expand_sum = third_sum(grid, *expand_quarters.second(expand_quarters.first(expand_grad)))
    second_got = grid.swap_core(second_other)
    back_middle, back_one, back_other, *joint_grad = attend_back(
        meta, small, middle, tokens_own, cot, item_got, part, part_got, mixed, output, output_got,
        normed, projected, attention, expand_bias, joint, joint_quarters,
    )
    joint_first = joint_quarters.first(joint_grad)
    joint_sum_all = third_sum(grid, *joint_quarters.second(joint_first))
    back_got = grid.swap_core(back_other)
    result, input_grad = finish(
        meta, small, tokens_own, middle, second, second_got, back_middle, back_one, back_got
    )
    gains_count = norm_gains.shape[1]

    third = [joint_sum_all[:, part_at * half : (part_at + 1) * half] for part_at in range(3)]
    small_part = joint_sum_all[:, 4 * half :]
    got = grid.swap_core(
        jnp.concatenate([jnp.where(core == 0, third[2], third[0]), small_part], axis=1)
    )
    joint_got = got[:, :half]
    small_own = (small_part + got[:, half:])[:, :small_rows].T
    joint_sum = jnp.where(
        core == 0,
        jnp.concatenate([third[0], joint_got, third[1]], axis=1),
        jnp.concatenate([third[1], joint_got, third[2]], axis=1),
    )
    output_sum = joint_sum_all[:, 3 * half : 4 * half]
    owner = grid.top == core
    side = shrink_sum.shape[1] // 2
    shrink_send = lax.dynamic_slice_in_dim(shrink_sum, (1 - core) * side, side, axis=1)
    shrink_keep = lax.dynamic_slice_in_dim(shrink_sum, core * side, side, axis=1)
    shrink_own = jnp.where(owner, shrink_keep, grid.swap_core(shrink_send))

    masters = (
        master_joint,
        master_output,
        master_expand,
        master_shrink,
        master_gains,
        master_biases,
    )
    firsts = (first_joint, first_output, first_expand, first_shrink, first_gains, first_biases)
    seconds = (
        second_joint,
        second_output,
        second_expand,
        second_shrink,
        second_gains,
        second_biases,
    )
    totals_all = (
        joint_sum[None],
        output_sum[None],
        expand_sum[None],
        shrink_own[None],
        small_own[None, :gains_count],
        small_own[None, gains_count:small_rows],
    )
    results = [result[None], input_grad[None]]
    for group_index in range(6):
        group_rate = learning_rate if group_index < 4 else small_rate
        new_master, new_first, new_second, new_copy = adamw(
            masters[group_index],
            firsts[group_index],
            seconds[group_index],
            totals_all[group_index],
            group_rate,
        )
        results.extend([totals_all[group_index], new_master, new_first, new_second, new_copy])
    return tuple(results)


def solution(mesh):
    placed = (
        P(("dp", "fsdp"), None, None),
        P(("dp", "fsdp"), None, None),
        P(("dp", "fsdp"), None),
        P(None, "fsdp", None),
        P(None, "fsdp", None),
        P(None, "fsdp", None),
        P(None, "fsdp", None),
        P(None, None, "fsdp"),
        P(None, None, "fsdp"),
        P(None, "fsdp", "dp"),
        P(None, "fsdp", "dp"),
        P(None, "fsdp", "dp"),
        P(None, "fsdp", "dp"),
        P(None, None, "fsdp"),
        P(None, None, "fsdp"),
        P(None, "fsdp", "dp"),
        P(None, "fsdp", "dp"),
        P(None, "fsdp", "dp"),
        P(None, "fsdp", "dp"),
        P(None, None, "fsdp"),
        P(None, None, "fsdp"),
        P(None, "fsdp", "dp"),
        P(None, "fsdp", "dp"),
        P(None, "fsdp", "dp"),
        P(None, "fsdp", "dp"),
        P(None, None, "fsdp"),
        P(None, None, "fsdp"),
    )
    return jax.shard_map(
        local,
        mesh=mesh,
        in_specs=placed,
        out_specs=(
            P(("dp", "fsdp"), None, None),
            P(("dp", "fsdp"), None, None),
            P(None, "fsdp", "dp"),
            P(None, "fsdp", "dp"),
            P(None, "fsdp", "dp"),
            P(None, "fsdp", "dp"),
            P(None, "fsdp", "dp"),
            P(None, "fsdp", "dp"),
            P(None, "fsdp", "dp"),
            P(None, "fsdp", "dp"),
            P(None, "fsdp", "dp"),
            P(None, "fsdp", "dp"),
            P(None, "fsdp", "dp"),
            P(None, "fsdp", "dp"),
            P(None, "fsdp", "dp"),
            P(None, "fsdp", "dp"),
            P(None, "fsdp", "dp"),
            P(None, "fsdp", "dp"),
            P(None, "fsdp", "dp"),
            P(None, "fsdp", "dp"),
            P(None, "fsdp", "dp"),
            P(None, "fsdp", "dp"),
            P(None, None, "fsdp"),
            P(None, None, "fsdp"),
            P(None, None, "fsdp"),
            P(None, None, "fsdp"),
            P(None, None, "fsdp"),
            P(None, None, "fsdp"),
            P(None, None, "fsdp"),
            P(None, None, "fsdp"),
            P(None, None, "fsdp"),
            P(None, None, "fsdp"),
        ),
        check_vma=False,
    )
```

```python
import jax
import jax.numpy as jnp
from jax import lax
from jax.experimental import pallas as pl
from jax.experimental.pallas import tpu as pltpu
from jax.sharding import PartitionSpec as P

HEAD_DIM = 64
STEP_COUNT = 3


beta_one = 0.5
beta_two = 0.5
learning_rate = 0.02
small_rate = 0.25
weight_decay = 0.1
epsilon = 1e-08
norm_epsilon = 1e-05
curve = 0.7978845608028654
cubic = 0.044715
half_type = jnp.bfloat16
wide = jnp.float32


def matmul(left, right):
    return lax.dot_general(left, right, (((1,), (0,)), ((), ())), preferred_element_type=wide)


def outer_sum(left, right):
    return lax.dot_general(left, right, (((0,), (0,)), ((), ())), preferred_element_type=wide)


def times_back(left, right):
    return lax.dot_general(left, right, (((1,), (1,)), ((), ())), preferred_element_type=wide)


def norm_parts(stream):
    centred = stream - jnp.mean(stream, axis=-1, keepdims=True)
    spread = jnp.mean(centred * centred, axis=-1, keepdims=True)
    scale = lax.rsqrt(spread + norm_epsilon)
    return centred * scale, scale


def norm_back(unit, scale, gain, upstream):
    inner = upstream * gain
    mean_inner = jnp.mean(inner, axis=-1, keepdims=True)
    mean_cross = jnp.mean(inner * unit, axis=-1, keepdims=True)
    return scale * (inner - mean_inner - unit * mean_cross)


def after(value, *others):
    return lax.optimization_barrier((value, *others))[0]


class Grid:
    def __init__(self):
        self.size = lax.axis_size("fsdp")
        self.index = lax.axis_index("fsdp")
        self.core = lax.axis_index("dp")
        bits = self.size.bit_length() - 1
        side = bits // 3
        x_bits = tuple(range(side))
        y_bits = tuple(range(side, 2 * side))
        self.orders = (x_bits + y_bits, y_bits + x_bits)
        self.steps = 2 * side
        self.low_bits = tuple(range(2 * side, bits - 1))
        self.top_bit = bits - 1
        self.top = self.index >> self.top_bit

    def swap(self, value, bit):
        return lax.ppermute(value, "fsdp", [(i, i ^ (1 << bit)) for i in range(self.size)])

    def swap_step(self, value, step):
        pairs = []
        for core in range(2):
            bit = self.orders[core][step]
            for i in range(self.size):
                pairs.append((core * self.size + i, core * self.size + (i ^ (1 << bit))))
        return lax.ppermute(value, ("dp", "fsdp"), pairs)

    def swap_core(self, value):
        return lax.ppermute(value, "dp", [(0, 1), (1, 0)])

    def swap_owned(self, value, bit, owned):
        pairs = []
        for core in range(2):
            for i in range(self.size):
                if ((i >> self.top_bit) == core) == owned:
                    pairs.append((core * self.size + i, core * self.size + (i ^ (1 << bit))))
        return lax.ppermute(value, ("dp", "fsdp"), pairs)

    def flip_step(self, rels, step):
        masks = [1 << self.orders[core][step] for core in range(2)]
        return tuple((rel[0] ^ masks[0], rel[1] ^ masks[1]) for rel in rels)


def flip_bit(rels, bit):
    return tuple((rel[0] ^ (1 << bit), rel[1] ^ (1 << bit)) for rel in rels)


class Gather:
    def __init__(self, grid, block, owned):
        self.grid, self.owned = grid, owned
        self.value, self.rels = block[None], ((0, 0),)
        self.done, self.last = [], None

    def high(self):
        grid = self.grid
        if self.owned:
            got = grid.swap_owned(self.value, grid.top_bit, True)
            self.value = jnp.where(grid.top == grid.core, self.value, got)
        else:
            got = grid.swap(self.value, grid.top_bit)
            self.value = jnp.concatenate([self.value, got], axis=0)
            self.rels = self.rels + flip_bit(self.rels, grid.top_bit)

    def low(self, apart):
        grid = self.grid
        self.start = [(self.rels, self.value)]
        for bit in grid.low_bits:
            self.start += [
                (flip_bit(rels, bit), grid.swap(value, bit)) for rels, value in self.start
            ]
        if not apart:
            rels = sum((rels for rels, _ in self.start), ())
            self.start = [(rels, jnp.concatenate([value for _, value in self.start], axis=0))]

    def first(self, which):
        grid = self.grid
        rels, value = self.start[which]
        one = (grid.flip_step(rels, 0), grid.swap_step(value, 0))
        middle = grid.steps // 2
        two = (grid.flip_step(rels, middle), grid.swap_step(value, middle))
        return [(rels, value), one], two

    def second(self, state):
        grid = self.grid
        pieces, early = state
        middle = grid.steps // 2
        for step in range(1, grid.steps):
            new = []
            for place, (rels, value) in enumerate(pieces):
                if step == middle and place == 0:
                    new.append(early)
                else:
                    new.append((grid.flip_step(rels, step), grid.swap_step(value, step)))
            pieces = pieces + new
        return pieces


def pick(rel, core):
    return jnp.where(core == 0, rel[0], rel[1])


def assemble(grid, pieces, count):
    rows, width = pieces[0][1].shape[1:]
    whole = jnp.zeros((count, rows, width), pieces[0][1].dtype)
    for rels, piece in pieces:
        for place, rel in enumerate(rels):
            spot = (grid.index ^ pick(rel, grid.core)) & (count - 1)
            whole = lax.dynamic_update_slice(whole, piece[place : place + 1], (spot, 0, 0))
    return whole.reshape(count * rows, width)


def adamw(master, first, second, gradient, rate):
    first_new = beta_one * first + (1.0 - beta_one) * gradient
    second_new = beta_two * second + (1.0 - beta_two) * gradient * gradient
    first_hat = first_new / (1.0 - beta_one**STEP_COUNT)
    second_hat = second_new / (1.0 - beta_two**STEP_COUNT)
    master_new = master - rate * (
        first_hat / (jnp.sqrt(second_hat) + epsilon) + weight_decay * master
    )
    return (master_new, first_new, second_new, master_new.astype(jnp.bfloat16))


RAW, HELD, FETCH, PUT, SCALAR = "raw", "held", "fetch", "put", "scalar"
SPACES = {RAW: pl.ANY, HELD: pltpu.VMEM, FETCH: pl.ANY, PUT: pl.ANY, SCALAR: pltpu.SMEM}


def shaped(shape, dtype):
    return jax.ShapeDtypeStruct(shape, dtype)


class Fetched:
    def __init__(self, copy, room):
        self.copy, self.room, self.waited = copy, room, False

    def ready(self):
        if not self.waited:
            self.copy.wait()
            self.waited = True
        return self.room


def call(body, name, operands, kinds, outs, out_kinds, scratch):
    moved = [o for o, kind in zip(operands, kinds) if kind == FETCH]
    moved += [o for o, kind in zip(outs, out_kinds) if kind == PUT]
    rooms = [pltpu.VMEM(o.shape, o.dtype) for o in moved]
    scratch = list(scratch)

    def whole(*refs):
        ins = refs[: len(operands)]
        results = refs[len(operands) : len(operands) + len(outs)]
        own = refs[len(operands) + len(outs) :]
        own, rest = own[: len(scratch)], own[len(scratch) :]
        room = list(rest[: len(moved)])
        sems = rest[len(moved)] if moved else None
        taken, arrived, written, puts = 0, [], [], []
        for ref, kind in zip(ins, kinds):
            if kind == FETCH:
                copy = pltpu.make_async_copy(ref, room[taken], sems.at[taken])
                copy.start()
                arrived.append(Fetched(copy, room[taken]))
                taken += 1
            else:
                arrived.append(ref)
        for ref, kind in zip(results, out_kinds):
            if kind == PUT:
                puts.append(pltpu.make_async_copy(room[taken], ref, sems.at[taken]))
                written.append(room[taken])
                taken += 1
            else:
                written.append(ref)
        body(*arrived, *written, *own)
        for ref in arrived:
            if isinstance(ref, Fetched):
                ref.ready()
        start_all(puts)
        wait_all(puts)

    return pl.pallas_call(
        whole,
        name=name,
        out_shape=tuple(outs),
        in_specs=[pl.BlockSpec(memory_space=SPACES[kind]) for kind in kinds],
        out_specs=tuple(pl.BlockSpec(memory_space=SPACES[kind]) for kind in out_kinds),
        scratch_shapes=scratch
        + rooms
        + ([pltpu.SemaphoreType.DMA((len(moved),))] if moved else []),
        compiler_params=pltpu.CompilerParams(vmem_limit_bytes=(60 if name == "pack_blocks" else 28) << 20),
        cost_estimate=pl.CostEstimate(flops=int({'pack_blocks': 1.5, 'attend': 4.3, 'grow': 9.5, 'shrink_back': 6.4, 'expand_grads': 4.3, 'attend_back': 9.0, 'finish': 2.6, 'update_small': 1.5}[name] * 1150000000), bytes_accessed=1, transcendentals=0),
    )(*operands)


class Layout:
    def __init__(self, count, rows, width):
        self.count, self.rows, self.width = count, rows, width
        self.direct = rows % 16 == 0

    def offset(self, index, core, rel):
        if rel[0] == rel[1]:
            spot = (index ^ rel[0]) & (self.count - 1)
        else:
            spot = (index ^ jnp.where(core == 0, rel[0], rel[1])) & (self.count - 1)
        return pl.multiple_of(spot * self.rows, 16)


class Loading:
    def __init__(self, pieces, refs, meta_ref, scratch):
        self.pieces, self.meta = pieces, meta_ref
        self.whole, self.room, self.sems = scratch
        self.copies, at = [], 0
        for place, ref in enumerate(refs):
            target = self.whole
            if pieces.rel_sets is not None:
                target = self.room.at[pl.ds(at, ref.shape[0])]
                at += ref.shape[0]
            self.copies.append(pltpu.make_async_copy(ref, target, self.sems.at[place]))
        start_all(self.copies)

    def ready(self):
        wait_all(self.copies)
        layout = self.pieces.layout
        if self.pieces.rel_sets is not None:
            rels = sum(self.pieces.rel_sets, ())
            for place, rel in enumerate(rels):
                spot = layout.offset(self.meta[0], self.meta[1], rel)
                self.whole[pl.ds(spot, layout.rows)] = self.room[place]
        return self.whole


class Storing:
    def __init__(self, parts, refs, meta_ref, scratch):
        self.parts, self.refs, self.meta = parts, refs, meta_ref
        self.room, self.sems = scratch
        self.copies = []

    def put(self, start, columns, value):
        layout = self.parts.layout
        value = value.astype(half_type)
        if not layout.direct:
            self.room[start : start + value.shape[0], columns] = value
            return
        for at in range(0, value.shape[0], layout.rows):
            place = self.parts.place((start + at) // layout.rows, self.meta)
            self.room[place, :, columns] = value[at : at + layout.rows]

    def send(self):
        if not self.parts.layout.direct:
            self.copies = [pltpu.make_async_copy(self.room, self.refs[0], self.sems.at[0])]
        else:
            quarter = self.parts.layout.count // 4
            starts = (2 * quarter, quarter, 0)
            self.copies = [
                pltpu.make_async_copy(
                    self.room.at[pl.ds(at, ref.shape[0])], ref, self.sems.at[place]
                )
                for place, (ref, at) in enumerate(zip(self.refs, starts))
            ]
        start_all(self.copies)

    def wait(self):
        wait_all(self.copies)


def start_all(copies):
    for copy in copies:
        copy.start()


def wait_all(copies):
    for copy in copies:
        copy.wait()


class Pieces:
    def __init__(self, grid, pieces, count):
        rows, width = pieces[0][1].shape[1:]
        self.layout = Layout(count, rows, width)
        if self.layout.direct:
            self.rel_sets = [rels for rels, _ in pieces]
            self.arrays = [piece for _, piece in pieces]
        else:
            self.rel_sets = None
            self.arrays = [assemble(grid, pieces, count)]

    def scratch(self):
        count, rows, width = self.layout.count, self.layout.rows, self.layout.width
        room = (count, rows, width) if self.rel_sets is not None else (1, 16, 128)
        return [
            pltpu.VMEM((count * rows, width), half_type),
            pltpu.VMEM(room, half_type),
            pltpu.SemaphoreType.DMA((len(self.arrays),)),
        ]


class Parts:
    def __init__(self, grid, layout, lasting):
        self.grid, self.layout = grid, layout
        count = layout.count
        self.bits = bits = [[*grid.orders[core], *lasting] for core in range(2)]
        rels = []
        for place in range(count):
            taken = [(place >> at) & 1 for at in range(len(bits[0]))][::-1]
            rels.append(
                tuple(
                    sum(1 << bit for bit, take in zip(bits[core], taken) if take)
                    for core in range(2)
                )
            )
        self.rels = tuple(rels)
        quarter = count // 4
        self.rel_sets = [rels[2 * quarter :], rels[quarter : 2 * quarter], rels[:quarter]]

    def shapes(self):
        rows, width = self.layout.rows, self.layout.width
        if self.layout.direct:
            return [shaped((len(rels), rows, width), half_type) for rels in self.rel_sets]
        return [shaped((self.layout.count * rows, width), half_type)]

    def scratch(self):
        count, rows, width = self.layout.count, self.layout.rows, self.layout.width
        shape = (count, rows, width) if self.layout.direct else (count * rows, width)
        return [pltpu.VMEM(shape, half_type), pltpu.SemaphoreType.DMA((3,))]

    def place(self, block, meta_ref):
        rel = (meta_ref[0] ^ block) & (self.layout.count - 1)
        spots = []
        for order in self.bits:
            last = len(order) - 1
            spots.append(sum(((rel >> bit) & 1) << (last - at) for at, bit in enumerate(order)))
        return jnp.where(meta_ref[1] == 0, spots[0], spots[1])

    def split_up(self, arrays):
        if self.layout.direct:
            return arrays
        grid, count = self.grid, self.layout.count
        blocks = arrays[0].reshape(count, self.layout.rows, self.layout.width)
        order = jnp.stack([(grid.index ^ pick(rel, grid.core)) & (count - 1) for rel in self.rels])
        blocks = jnp.take(blocks, order, axis=0, mode="clip")
        return blocks[count // 2 :], blocks[count // 4 : count // 2], blocks[: count // 4]

    def first(self, arrays):
        send, next_send, keep = self.split_up(arrays)
        got = self.grid.swap_step(send, 0)
        middle = got.shape[0] // 2
        return join(next_send, got[middle:]), join(keep, got[:middle])

    def second(self, state):
        send, keep = state
        for step in range(1, self.grid.steps):
            got = self.grid.swap_step(send, step)
            if step == self.grid.steps - 1:
                return keep, got
            middle = keep.shape[0] // 2
            send, keep = join(keep[middle:], got[middle:]), join(keep[:middle], got[:middle])


def join(keep, got):
    return (keep.astype(wide) + got.astype(wide)).astype(half_type)


def third_sum(grid, keep, got, owned=False):
    near, far = keep, got
    for bit in grid.low_bits[::-1]:
        middle = near.shape[0] // 2
        send, near = join(near[middle:], far[middle:]), join(near[:middle], far[:middle])
        far = grid.swap(send, bit)
    if owned:
        last = grid.swap_owned(join(near, far), grid.top_bit, False)
    else:
        middle = near.shape[0] // 2
        last = grid.swap(join(near[middle:], far[middle:]), grid.top_bit)
        near, far = near[:middle], far[:middle]
    return (near.astype(wide) + far.astype(wide) + last.astype(wide))[0]


def pack_blocks(meta, lengths, tokens, cot, joint, output, expand, gains, biases):
    rows = joint.shape[0]
    count, width = tokens.shape
    half = width // 2
    hidden = expand.shape[1] // 2
    small = gains.shape[0] + biases.shape[0]

    def body(meta_ref, lengths_ref, tokens_ref, cot_ref, joint_ref, output_ref, expand_ref, gain_ref, bias_ref, one_ref, two_ref, item_ref, room):
        core = meta_ref[1]
        side = pl.multiple_of(core * half, 128)
        gains_count = gain_ref.room.shape[0]
        room[...] = jnp.zeros_like(room)
        room[:gains_count, :rows] = gain_ref.ready()[...].astype(wide)
        room[gains_count:small, :rows] = bias_ref.ready()[...].astype(wide)
        one_ref[:, 4 * half :] = room[...].T[:rows].astype(half_type)
        mat = joint_ref.ready()
        for part in range(3):
            one_ref[:, part * half : (part + 1) * half] = mat[
                :, pl.ds(pl.multiple_of(part * width + side, 128), half)
            ]
        one_ref[:, 3 * half : 4 * half] = output_ref.ready()[:, pl.ds(side, half)]
        two_ref[...] = expand_ref.ready()[:, pl.ds(pl.multiple_of(core * hidden, 128), hidden)]
        line = (16, width)
        lane = lax.broadcasted_iota(jnp.int32, line, 1)
        value = jnp.where(lane == 0, lengths_ref[0], jnp.where(lane == 1, lengths_ref[1], 0))
        item_ref[:count] = tokens_ref.ready()[...]
        item_ref[count : 2 * count] = cot_ref.ready()[...]
        item_ref[2 * count :] = value.astype(wide).astype(half_type)

    return call(
        body,
        "pack_blocks",
        (meta, lengths, tokens, cot, joint, output, expand, gains, biases),
        (SCALAR, SCALAR) + (FETCH,) * 7,
        (
            shaped((rows, 4 * half + 128), half_type),
            shaped((rows, hidden), half_type),
            shaped((2 * count + 16, width), half_type),
        ),
        (PUT, PUT, PUT),
        (pltpu.VMEM((128, 128), wide),),
    )


def lane_is_low(shape):
    return lax.broadcasted_iota(jnp.int32, shape, 1) < HEAD_DIM


def two_heads(value, low):
    zero = jnp.zeros_like(value)
    return jnp.concatenate([jnp.where(low, value, zero), jnp.where(low, zero, value)], axis=0)


def one_of_two(value, low):
    rows = value.shape[0] // 2
    return jnp.where(low, value[:rows], value[rows:])


def attend(meta, lengths, tokens, item_got, joint):
    tokens_rows, width = tokens.shape
    half = width // 2
    rows = 2 * tokens_rows
    pairs = half // 128

    def body(meta_ref, lengths_ref, own_ref, item_ref, *rest):
        pieces = rest[: len(joint.arrays)]
        normed_ref, projected_ref, attention_ref, attended_ref, output_ref, small_ref = rest[
            len(joint.arrays) : len(joint.arrays) + 6
        ]
        core = meta_ref[1]
        loading = Loading(joint, pieces, meta_ref, rest[len(joint.arrays) + 6 :])
        sides = (own_ref.ready()[...], item_ref.ready()[:tokens_rows])
        units = [norm_parts(side.astype(wide))[0] for side in sides]
        mat = loading.ready()
        small_ref[...] = mat[:, 4 * half :].astype(wide).T[:16]
        output_ref[...] = mat[:, 3 * half : 4 * half]
        side = pl.multiple_of(core * half, 128)
        for item in range(2):
            normed_ref[item * tokens_rows : (item + 1) * tokens_rows] = (
                units[item] * small_ref[0:1] + small_ref[2:3]
            ).astype(half_type)
        normed = normed_ref[...]
        for part in range(3):
            spot = slice(part * half, (part + 1) * half)
            value = matmul(normed, mat[:, spot])
            if part != 1:
                row = 4 if part == 0 else 5
                value = value + small_ref[row : row + 1, pl.ds(side, half)]
            projected_ref[:, spot] = value.astype(half_type)
        low = lane_is_low((tokens_rows, 128))
        query = lax.broadcasted_iota(jnp.int32, (rows, tokens_rows), 0) % tokens_rows
        key = lax.broadcasted_iota(jnp.int32, (rows, tokens_rows), 1)
        for item in range(2):
            if item == 0:
                prefix, total = lengths_ref[0], lengths_ref[1]
            else:
                line = item_ref.room[2 * tokens_rows : 2 * tokens_rows + 16].astype(wide)
                prefix = line[0:1, 0:1].astype(jnp.int32)
                total = line[0:1, 1:2].astype(jnp.int32)
            visible = (key < total) & ((key <= query) | (key < prefix))
            take = slice(item * tokens_rows, (item + 1) * tokens_rows)
            for pair in range(pairs):
                spot = slice(pair * 128, (pair + 1) * 128)
                queries = two_heads(projected_ref[take, spot], low)
                keys = projected_ref[take, half + pair * 128 : half + (pair + 1) * 128]
                values = projected_ref[take, 2 * half + pair * 128 : 2 * half + (pair + 1) * 128]
                scores = times_back(queries, keys) * HEAD_DIM ** (-0.5)
                scores = jnp.where(visible, scores, -1e30)
                powers = jnp.exp(scores - jnp.max(scores, axis=-1, keepdims=True))
                attention = powers / jnp.sum(powers, axis=-1, keepdims=True)
                attention_ref[item * pairs + pair] = attention
                mixed = matmul(attention.astype(half_type), values)
                attended_ref[take, spot] = one_of_two(mixed, low).astype(half_type)

    return call(
        body,
        "attend",
        (meta, lengths, tokens, item_got, *joint.arrays),
        (SCALAR, SCALAR, FETCH, FETCH) + (RAW,) * len(joint.arrays),
        (
            shaped((rows, width), half_type),
            shaped((rows, 3 * half), half_type),
            shaped((2 * pairs, rows, tokens_rows), wide),
            shaped((rows, half), half_type),
            shaped((width, half), half_type),
            shaped((16, width), wide),
        ),
        (HELD, HELD, HELD, PUT, PUT, HELD),
        joint.scratch(),
    )


def flipped(ref):
    rows = ref.shape[0] // 2
    return jnp.concatenate([ref[rows:], ref[:rows]], axis=0)


def grow(meta, small, tokens, cot, item_got, attended, attended_got, output, output_got, expand, quarters):
    tokens_rows, width = tokens.shape
    half = width // 2
    rows = 2 * tokens_rows
    hidden = expand.layout.width
    shapes = quarters.shapes()
    step = 384

    def body(meta_ref, small_ref, own_ref, cot_ref, item_ref, attended_ref, attended_got_ref, output_ref, output_got_ref, *rest):
        pieces = rest[: len(expand.arrays)]
        rest = rest[len(expand.arrays) :]
        middle_ref, normed_ref, active_ref, slope_ref, mixed_ref = rest[:5]
        grads = rest[5 : 5 + len(shapes)]
        *scratch, upstream = rest[5 + len(shapes) :]
        core = meta_ref[1]
        loading = Loading(expand, pieces, meta_ref, scratch[:3])
        storing = Storing(quarters, grads, meta_ref, scratch[3:])
        mine = pl.ds(pl.multiple_of(core * half, 128), half)
        yours = pl.ds(pl.multiple_of((1 - core) * half, 128), half)
        mixed_ref[:, mine] = attended_ref.ready()[...]
        mixed_ref[:, yours] = flipped(attended_got_ref.ready())
        mixed = mixed_ref[...]
        middle_ref[:, mine] = matmul(mixed, output_ref.ready()[...])
        middle_ref[:, yours] = matmul(mixed, output_got_ref.ready()[...])
        sides = (own_ref.ready()[...], item_ref.ready()[:tokens_rows])
        for item, side in enumerate(sides):
            take = slice(item * tokens_rows, (item + 1) * tokens_rows)
            middle = side.astype(wide) + (middle_ref[take] + small_ref[6:7])
            middle_ref[take] = middle
            unit, _ = norm_parts(middle)
            normed_ref[take] = (unit * small_ref[1:2] + small_ref[3:4]).astype(half_type)
        upstream[:tokens_rows] = cot_ref.ready()[...]
        upstream[tokens_rows:] = item_ref.ready()[tokens_rows : 2 * tokens_rows]
        mat = loading.ready()
        normed = normed_ref[...]
        back = upstream[...]
        for at in range(0, hidden, step):
            spot = slice(at, at + step)
            row = 8 + core * (hidden // width) + at // width
            bias = small_ref[pl.ds(row, 1), at % width : at % width + step]
            value = matmul(normed, mat[:, spot]) + bias
            square = value * value
            bent = jnp.tanh(curve * (value + cubic * value * square))
            active = (0.5 * value * (1.0 + bent)).astype(half_type)
            active_ref[:, spot] = active
            slope_ref[:, spot] = 0.5 * (1.0 + bent) + 0.5 * value * (1.0 - bent * bent) * (
                curve * (1.0 + 3.0 * cubic * square)
            )
            storing.put(at, slice(None), outer_sum(active, back))
        storing.send()
        storing.wait()

    outs = (
        shaped((rows, width), wide),
        shaped((rows, width), half_type),
        shaped((rows, hidden), half_type),
        shaped((rows, hidden), wide),
        shaped((rows, width), half_type),
    ) + tuple(shapes)
    return call(
        body,
        "grow",
        (meta, small, tokens, cot, item_got, attended, attended_got, output, output_got, *expand.arrays),
        (SCALAR, HELD) + (FETCH,) * 7 + (RAW,) * len(expand.arrays),
        outs,
        (HELD,) * 5 + (RAW,) * len(shapes),
        (*expand.scratch(), *quarters.scratch(), pltpu.VMEM((rows, width), half_type)),
    )


def shrink_back(meta, cot, item_got, slope, active, shrink, expand):
    tokens_rows, width = cot.shape
    rows = 2 * tokens_rows
    hidden = expand.layout.width

    def body(meta_ref, cot_ref, item_ref, slope_ref, active_ref, *rest):
        shrink_pieces = rest[: len(shrink.arrays)]
        rest = rest[len(shrink.arrays) :]
        expand_pieces = rest[: len(expand.arrays)]
        hidden_ref, part_ref, second_ref, other_ref, *scratch, upstream = rest[len(expand.arrays) :]
        first = Loading(shrink, shrink_pieces, meta_ref, scratch[:3])
        second = Loading(expand, expand_pieces, meta_ref, scratch[3:])
        upstream[:tokens_rows] = cot_ref.ready()[...]
        upstream[tokens_rows:] = item_ref.ready()[tokens_rows : 2 * tokens_rows]
        mat = first.ready()
        step = 384
        for at in range(0, hidden, step):
            spot = slice(at, at + step)
            value = times_back(upstream[...], mat[spot])
            hidden_ref[:, spot] = (value * slope_ref[:, spot]).astype(half_type)
        for ref, at in ((second_ref, 0), (other_ref, tokens_rows)):
            ref[...] = matmul(active_ref[at : at + tokens_rows], mat[...])
        other = second.ready()
        part_ref[...] = times_back(hidden_ref[...], other[...])

    return call(
        body,
        "shrink_back",
        (meta, cot, item_got, slope, active, *shrink.arrays, *expand.arrays),
        (SCALAR, FETCH, FETCH, HELD, HELD) + (RAW,) * (len(shrink.arrays) + len(expand.arrays)),
        (
            shaped((rows, hidden), half_type),
            shaped((rows, width), wide),
            shaped((tokens_rows, width), wide),
            shaped((tokens_rows, width), wide),
        ),
        (HELD, PUT, HELD, PUT),
        (*shrink.scratch(), *expand.scratch(), pltpu.VMEM((rows, width), half_type)),
    )


def expand_grads(meta, normed_two, back_hidden, quarters):
    width = normed_two.shape[1]
    hidden = back_hidden.shape[1]
    shapes = quarters.shapes()

    def body(meta_ref, normed_ref, hidden_ref, bias_ref, *rest):
        storing = Storing(quarters, rest[: len(shapes)], meta_ref, rest[len(shapes) :])
        step = 384
        for at in range(0, hidden, step):
            spot = slice(at, at + step)
            storing.put(0, spot, outer_sum(normed_ref[...], hidden_ref[:, spot]))
        storing.send()
        bias_ref[...] = jnp.sum(hidden_ref[...].astype(wide), axis=0, keepdims=True)
        storing.wait()

    return call(
        body,
        "expand_grads",
        (meta, normed_two, back_hidden),
        (SCALAR, HELD, HELD),
        (shaped((1, hidden), wide),) + tuple(shapes),
        (HELD,) + (RAW,) * len(shapes),
        quarters.scratch(),
    )


def attend_back(meta, small, middle, tokens, cot, item_got, part, part_got, mixed, output, output_got, normed, projected, attention, expand_bias, joint, quarters):
    rows, width = middle.shape
    half = width // 2
    tokens_rows = rows // 2
    pairs = half // 128
    shapes = quarters.shapes()

    def body(meta_ref, small_ref, middle_ref, tokens_ref, cot_ref, item_ref, part_ref, part_got_ref, mixed_ref, output_ref, output_got_ref, normed_ref, projected_ref, attention_ref, bias_ref, *rest):
        pieces = rest[: len(joint.arrays)]
        rest = rest[len(joint.arrays) :]
        back_middle_ref, own_ref, other_ref = rest[:3]
        grads = rest[3 : 3 + len(shapes)]
        *scratch, branch, back_projected_ref, sums_ref = rest[3 + len(shapes) :]
        core = meta_ref[1]
        loading = Loading(joint, pieces, meta_ref, scratch[:3])
        storing = Storing(quarters, grads, meta_ref, scratch[3:])
        mine = pl.ds(pl.multiple_of(core * half, 128), half)
        yours = pl.ds(pl.multiple_of((1 - core) * half, 128), half)
        gain = jnp.zeros((1, width), wide)
        shift = jnp.zeros((1, width), wide)
        bias_branch = jnp.zeros((1, width), wide)
        bias_second = jnp.zeros((1, width), wide)
        sides = (cot_ref.ready()[...], item_ref.ready()[tokens_rows : 2 * tokens_rows])
        part_ref, part_got_ref = part_ref.ready(), part_got_ref.ready()
        output_ref, output_got_ref = output_ref.ready(), output_got_ref.ready()
        for item, side in enumerate(sides):
            take = slice(item * tokens_rows, (item + 1) * tokens_rows)
            across = slice((1 - item) * tokens_rows, (2 - item) * tokens_rows)
            unit, scale = norm_parts(middle_ref[take])
            upstream = side.astype(wide)
            back = part_ref[take] + part_got_ref[across].astype(wide)
            value = upstream + norm_back(unit, scale, small_ref[1:2], back)
            if item == 0:
                back_middle_ref[...] = value
            low_value = value.astype(half_type)
            branch[take] = low_value
            gain = gain + jnp.sum(back * unit, axis=0, keepdims=True)
            shift = shift + jnp.sum(back, axis=0, keepdims=True)
            bias_branch = bias_branch + jnp.sum(low_value.astype(wide), axis=0, keepdims=True)
            bias_second = bias_second + jnp.sum(upstream, axis=0, keepdims=True)
        sums_ref[...] = jnp.zeros_like(sums_ref)
        sums_ref[1:2] = 0.5 * gain
        sums_ref[3:4] = 0.5 * shift
        sums_ref[6:7] = 0.5 * bias_branch
        sums_ref[7:8] = 0.5 * bias_second
        storing.put(0, slice(3 * half, 4 * half), outer_sum(mixed_ref[...], branch[:, mine]))
        height = pl.ds(pl.multiple_of(core * half, 128), half)
        back_attended = (
            times_back(branch[:, mine], output_ref[height])
            + times_back(branch[:, yours], output_got_ref[height])
        ).astype(half_type)
        low = lane_is_low((tokens_rows, 128))
        for item in range(2):
            take = slice(item * tokens_rows, (item + 1) * tokens_rows)
            for pair in range(pairs):
                spot = slice(pair * 128, (pair + 1) * 128)
                queries = two_heads(projected_ref[take, spot], low)
                keys = projected_ref[take, half + pair * 128 : half + (pair + 1) * 128]
                values = projected_ref[take, 2 * half + pair * 128 : 2 * half + (pair + 1) * 128]
                upstream = two_heads(back_attended[take, spot], low)
                attention = attention_ref[item * pairs + pair]
                back_values = outer_sum(attention.astype(half_type), upstream)
                back_attention = times_back(upstream, values)
                inner = jnp.sum(attention * back_attention, axis=-1, keepdims=True)
                back_scores = (HEAD_DIM ** (-0.5) * attention * (back_attention - inner)).astype(half_type)
                back_queries = one_of_two(matmul(back_scores, keys), low)
                back_keys = outer_sum(back_scores, queries)
                for part_at, value in enumerate((back_queries, back_keys, back_values)):
                    start = part_at * half + pair * 128
                    back_projected_ref[take, start : start + 128] = value.astype(half_type)
        sums_ref[4:5, mine] = jnp.sum(back_projected_ref[:, :half].astype(wide), axis=0, keepdims=True)
        sums_ref[5:6, mine] = jnp.sum(
            back_projected_ref[:, 2 * half :].astype(wide), axis=0, keepdims=True
        )
        for part_at in range(3):
            spot = slice(part_at * half, (part_at + 1) * half)
            storing.put(0, spot, outer_sum(normed_ref[...], back_projected_ref[:, spot]))
        mat = loading.ready()
        gain = jnp.zeros((1, width), wide)
        shift = jnp.zeros((1, width), wide)
        sides = (tokens_ref.ready()[...], item_ref.ready()[:tokens_rows])
        for item, (side, ref) in enumerate(zip(sides, (own_ref, other_ref))):
            take = slice(item * tokens_rows, (item + 1) * tokens_rows)
            back = times_back(back_projected_ref[take], mat[:, : 3 * half])
            ref[...] = back
            unit, _ = norm_parts(side.astype(wide))
            gain = gain + jnp.sum(back * unit, axis=0, keepdims=True)
            shift = shift + jnp.sum(back, axis=0, keepdims=True)
        sums_ref[0:1] = gain
        sums_ref[2:3] = shift
        count = bias_ref.shape[1] // width
        for at in range(count):
            sums_ref[pl.ds(8 + core * count + at, 1)] = bias_ref[:, at * width : (at + 1) * width]
        storing.put(0, slice(4 * half, 4 * half + 128), sums_ref[...].T)
        storing.send()
        storing.wait()

    outs = (
        shaped((tokens_rows, width), wide),
        shaped((tokens_rows, width), wide),
        shaped((tokens_rows, width), wide),
    ) + tuple(shapes)
    return call(
        body,
        "attend_back",
        (meta, small, middle, tokens, cot, item_got, part, part_got, mixed, output, output_got, normed, projected, attention, expand_bias, *joint.arrays),
        (SCALAR, HELD, HELD, FETCH, FETCH, FETCH, FETCH, FETCH, HELD, FETCH, FETCH, HELD, HELD, HELD, HELD) + (RAW,) * len(joint.arrays),
        outs,
        (HELD, HELD, PUT) + (RAW,) * len(shapes),
        (
            *joint.scratch(),
            *quarters.scratch(),
            pltpu.VMEM((rows, width), half_type),
            pltpu.VMEM((rows, 3 * half), half_type),
            pltpu.VMEM((128, width), wide),
        ),
    )


def finish(meta, small, tokens, middle, second, second_got, back_middle, back_one, back_got):
    tokens_rows, width = tokens.shape

    def body(meta_ref, small_ref, own_ref, middle_ref, second_ref, second_got_ref, back_middle_ref, back_ref, back_got_ref, result_ref, input_ref):
        result_ref[...] = middle_ref[:tokens_rows] + (
            second_ref[...] + second_got_ref.ready()[...] + small_ref[7:8]
        )
        unit, scale = norm_parts(own_ref.ready()[...].astype(wide))
        back = back_ref[...] + back_got_ref.ready()[...]
        input_ref[...] = back_middle_ref[...] + norm_back(unit, scale, small_ref[0:1], back)

    return call(
        body,
        "finish",
        (meta, small, tokens, middle, second, second_got, back_middle, back_one, back_got),
        (SCALAR, HELD, FETCH, HELD, HELD, FETCH, HELD, HELD, FETCH),
        (shaped((tokens_rows, width), wide), shaped((tokens_rows, width), wide)),
        (PUT, PUT),
        (),
    )


def update_small(meta, part, got, states):
    rows, width = part.shape
    shapes = []
    for value in states[::3]:
        shape = (value.shape[0], 1, rows)
        shapes += [shaped(shape, wide)] * 4 + [shaped(shape, half_type)]

    def body(meta_ref, part_ref, got_ref, *rest):
        held, outs, room = rest[:6], rest[6:16], rest[16]
        room[...] = jnp.zeros_like(room)
        room[:rows] = part_ref.ready()[...] + got_ref.ready()[...]
        small = room[...].T
        start = 0
        for at in range(2):
            values = [ref.ready()[...] for ref in held[3 * at : 3 * at + 3]]
            count = values[0].shape[0]
            gradient = small[start : start + count, :rows]
            start += count
            new = adamw(*values, gradient, small_rate)
            for ref, value in zip(outs[5 * at : 5 * at + 5], (gradient, *new)):
                ref[...] = value.reshape(ref.shape)

    return call(
        body,
        "update_small",
        (meta, part, got, *states),
        (SCALAR,) + (FETCH,) * 8,
        shapes,
        (PUT,) * 10,
        (pltpu.VMEM((width, width), wide),),
    )


def local(
    tokens,
    cotangent,
    lengths,
    joint_weight,
    output_weight,
    expand_weight,
    shrink_weight,
    norm_gains,
    bias_rows,
    master_joint,
    master_output,
    master_expand,
    master_shrink,
    master_gains,
    master_biases,
    first_joint,
    first_output,
    first_expand,
    first_shrink,
    first_gains,
    first_biases,
    second_joint,
    second_output,
    second_expand,
    second_shrink,
    second_gains,
    second_biases,
):
    grid = Grid()
    core = grid.core
    size = grid.size
    width = tokens.shape[2]
    half = width // 2
    meta = jnp.stack([grid.index, core])
    lengths_own = lengths[0]
    tokens_own, cot = tokens[0], cotangent[0]
    joint_block, expand_block, item = pack_blocks(
        meta, lengths_own, tokens_own, cot,
        joint_weight[0], output_weight[0], expand_weight[0], norm_gains[0], bias_rows[0],
    )
    item_got = grid.swap_core(item)
    one = Gather(grid, joint_block, False)
    two = Gather(grid, expand_block, False)
    three = Gather(grid, after(shrink_weight[0], joint_block), True)
    one.high()
    two.value = after(two.value, one.value)
    two.high()
    three.value = after(three.value, two.value)
    three.high()
    one.low(True)
    one_near = one.first(0)
    two.value = after(two.value, one_near[0][1][1], one_near[1][1], one.start[1][1])
    two.low(False)
    three.low(False)
    one.start[1] = (one.start[1][0], after(one.start[1][1], one_near[0][1][1], one_near[1][1]))
    one_far = one.first(1)
    near_pieces = one.second(one_near)
    one_far[0][1] = (one_far[0][1][0], after(one_far[0][1][1], *[piece for _, piece in near_pieces], one_far[1][1]))
    joint = Pieces(grid, near_pieces + one.second(one_far), size)
    two.start[0] = (two.start[0][0], after(two.start[0][1], one_far[0][1][1], one_far[1][1]))
    two_all = two.first(0)
    expand = Pieces(grid, two.second(two_all), size)
    three.start[0] = (three.start[0][0], after(three.start[0][1], two_all[0][1][1]))
    three_all = three.first(0)
    shrink = Pieces(grid, three.second(three_all), size // 2)
    lasting = (*grid.low_bits[::-1], grid.top_bit)
    shrink_quarters = Parts(grid, shrink.layout, lasting[:-1])
    expand_quarters = Parts(grid, expand.layout, lasting)
    joint_quarters = Parts(grid, Layout(size, joint.layout.rows, 4 * half + 128), lasting)

    normed, projected, attention, attended, output, small = attend(
        meta, lengths_own, tokens_own, item_got, joint
    )
    attended_got = after(
        grid.swap_core(after(attended, expand.arrays[-1])), three_all[0][1][1], three_all[1][1]
    )
    output_got = grid.swap_core(output)
    middle, normed_two, active, slope, mixed, *shrink_grads = grow(
        meta, small, tokens_own, cot, item_got, attended, attended_got,
        output, output_got, expand, shrink_quarters,
    )
    shrink_sum = third_sum(grid, *shrink_quarters.second(shrink_quarters.first(shrink_grads)), owned=True)
    back_hidden, part, second, second_other = shrink_back(
        meta, cot, item_got, slope, active, shrink, expand
    )
    part_got = grid.swap_core(part)
    expand_bias, *expand_grad = expand_grads(meta, normed_two, back_hidden, expand_quarters)
    expand_sum = third_sum(grid, *expand_quarters.second(expand_quarters.first(expand_grad)))
    second_got = grid.swap_core(second_other)
    back_middle, back_one, back_other, *joint_grad = attend_back(
        meta, small, middle, tokens_own, cot, item_got, part, part_got, mixed, output, output_got,
        normed, projected, attention, expand_bias, joint, joint_quarters,
    )
    joint_first = joint_quarters.first(joint_grad)
    joint_sum_all = third_sum(grid, *joint_quarters.second(joint_first))
    back_got = grid.swap_core(back_other)
    result, input_grad = finish(
        meta, small, tokens_own, middle, second, second_got, back_middle, back_one, back_got
    )

    third = [joint_sum_all[:, part_at * half : (part_at + 1) * half] for part_at in range(3)]
    small_part = joint_sum_all[:, 4 * half :]
    got = grid.swap_core(
        jnp.concatenate([jnp.where(core == 0, third[2], third[0]), small_part], axis=1)
    )
    joint_got = got[:, :half]
    small_results = update_small(
        meta,
        small_part,
        got[:, half:],
        [
            value[0]
            for value in (
                master_gains, first_gains, second_gains, master_biases, first_biases, second_biases,
            )
        ],
    )
    small_results = [jnp.transpose(value, (1, 0, 2)) for value in small_results]
    joint_sum = jnp.where(
        core == 0,
        jnp.concatenate([third[0], joint_got, third[1]], axis=1),
        jnp.concatenate([third[1], joint_got, third[2]], axis=1),
    )
    output_sum = joint_sum_all[:, 3 * half : 4 * half]
    owner = grid.top == core
    side = shrink_sum.shape[1] // 2
    shrink_send = lax.dynamic_slice_in_dim(shrink_sum, (1 - core) * side, side, axis=1)
    shrink_keep = lax.dynamic_slice_in_dim(shrink_sum, core * side, side, axis=1)
    shrink_own = jnp.where(owner, shrink_keep, grid.swap_core(shrink_send))

    results = [result[None], input_grad[None]]
    for total, master, first, second_moment in (
        (joint_sum, master_joint, first_joint, second_joint),
        (output_sum, master_output, first_output, second_output),
        (expand_sum, master_expand, first_expand, second_expand),
        (shrink_own, master_shrink, first_shrink, second_shrink),
    ):
        gradient = total[None]
        results += [gradient, *adamw(master, first, second_moment, gradient, learning_rate)]
    return tuple([*results, *small_results])


def solution(mesh):
    placed = (
        P(("dp", "fsdp"), None, None),
        P(("dp", "fsdp"), None, None),
        P(("dp", "fsdp"), None),
        P(None, "fsdp", None),
        P(None, "fsdp", None),
        P(None, "fsdp", None),
        P(None, "fsdp", None),
        P(None, None, "fsdp"),
        P(None, None, "fsdp"),
        P(None, "fsdp", "dp"),
        P(None, "fsdp", "dp"),
        P(None, "fsdp", "dp"),
        P(None, "fsdp", "dp"),
        P(None, None, "fsdp"),
        P(None, None, "fsdp"),
        P(None, "fsdp", "dp"),
        P(None, "fsdp", "dp"),
        P(None, "fsdp", "dp"),
        P(None, "fsdp", "dp"),
        P(None, None, "fsdp"),
        P(None, None, "fsdp"),
        P(None, "fsdp", "dp"),
        P(None, "fsdp", "dp"),
        P(None, "fsdp", "dp"),
        P(None, "fsdp", "dp"),
        P(None, None, "fsdp"),
        P(None, None, "fsdp"),
    )
    return jax.shard_map(
        local,
        mesh=mesh,
        in_specs=placed,
        out_specs=(
            P(("dp", "fsdp"), None, None),
            P(("dp", "fsdp"), None, None),
            P(None, "fsdp", "dp"),
            P(None, "fsdp", "dp"),
            P(None, "fsdp", "dp"),
            P(None, "fsdp", "dp"),
            P(None, "fsdp", "dp"),
            P(None, "fsdp", "dp"),
            P(None, "fsdp", "dp"),
            P(None, "fsdp", "dp"),
            P(None, "fsdp", "dp"),
            P(None, "fsdp", "dp"),
            P(None, "fsdp", "dp"),
            P(None, "fsdp", "dp"),
            P(None, "fsdp", "dp"),
            P(None, "fsdp", "dp"),
            P(None, "fsdp", "dp"),
            P(None, "fsdp", "dp"),
            P(None, "fsdp", "dp"),
            P(None, "fsdp", "dp"),
            P(None, "fsdp", "dp"),
            P(None, "fsdp", "dp"),
            P(None, None, "fsdp"),
            P(None, None, "fsdp"),
            P(None, None, "fsdp"),
            P(None, None, "fsdp"),
            P(None, None, "fsdp"),
            P(None, None, "fsdp"),
            P(None, None, "fsdp"),
            P(None, None, "fsdp"),
            P(None, None, "fsdp"),
            P(None, None, "fsdp"),
        ),
        check_vma=False,
    )
```
